32 devices in a mesh: freq: 2 (over y), row: 4 (over z), col: 4 (over x, core).
Axes of the slice: x: 2, y: 2, z: 4, core: 2. Of those that a mesh axis runs over, the one named last changes fastest.
Arguments:
- traces: bfloat16 [4, 6144, 6144], P('freq', 'row', 'col'), parts along dimension 0, may hold values from -6 to 6
- recv_live: int32 [12288], P('freq'), parts along dimension 0, may hold values 0 or 1
- missing: int32 [8, 96], P('freq'), parts along dimension 0, may hold values from 0 to 1535, as said below
- wavelet: float32 [4], P('freq'), parts along dimension 0, may hold values from 0.5 to 1.5
Outputs:
- primaries: float32 [4, 6144, 512], P('freq', 'row', 'col'), parts along dimension 0
The draws below stay inside these ranges and needn't reach their ends.
There are 2 independent parts, one for each index of `freq`. The reference program is written for one: setup_inputs(seed, part) draws one part's arguments, and reference() takes and returns one part's arrays. A program takes and returns all parts, laid end to end along the dimension named above; each array names one. Nothing has to cross between parts.
Inputs may be any that keep to these rules, and one draw needn't show every extreme that they name: `missing`: each row lists 96 distinct positions within one block of 1536 shots, the shots of that block that were not recorded; the block's first and last shots are always among them.
All inputs are finite; a program needn't handle non-finite values.
Results may differ from the reference program's by a relative error of at most 0.0003.
Values may be sent and summed in bfloat16 or wider, within the bound.
A program may use at most 128 MiB of HBM per device.

```python
import math
import jax
import jax.numpy as jnp
from jax import lax

ORDER = 6144
WIN = 128
MISS = 96
TILE = 1536
BLOCKS = 4
N_ROW = 4


def draw_missing(key, part):
    sub_keys = jax.random.split(key, BLOCKS)

    def one_block(sub_key):
        shuffled = jax.random.permutation(sub_key, TILE - 2)[:MISS - 2] + 1
        ends = jnp.array([0, TILE - 1], jnp.int32)
        return jnp.concatenate([ends, shuffled.astype(jnp.int32)])
    return jax.vmap(one_block)(sub_keys)


def set_ends(drawn, key, least, top_value):
    shape = drawn.shape
    index_at = [jax.random.randint(jax.random.fold_in(key, axis), (), 0, shape[axis]) for axis in range(len(shape))]
    drawn = drawn.at[tuple(index_at)].set(least)
    longest = shape.index(max(shape))
    index_at[longest] = (index_at[longest] + 1) % shape[longest]
    return drawn.at[tuple(index_at)].set(top_value)


def block_scale(key, shape, pieces, smallest, high):
    def one(position, blocks):
        heights = jax.random.uniform(jax.random.fold_in(jax.random.fold_in(key, 6), position), (blocks,), jnp.float32, smallest / len(pieces), high / len(pieces))
        return jnp.repeat(jnp.exp(heights), shape[position] // blocks).reshape((-1,) + (1,) * (len(shape) - position - 1))

    loudness = one(*pieces[0])
    for cut in pieces[1:]:
        loudness = loudness * one(*cut)
    return loudness


def centred(rng, shape, spread, limit, shards=(), held_as=jnp.bfloat16):
    gain = block_scale(rng, shape, shards, -0.22, 0.18) if shards else 1.0
    values = jax.random.normal(rng, shape, jnp.float32) * spread * gain
    return jnp.minimum(jnp.maximum(values, -limit), limit).astype(held_as)


def setup_inputs(seed: int = 0, part: int = 0) -> dict:
    arg_keys = jax.random.split(jax.random.key(seed), 5)
    part_keys = jax.random.split(jax.random.fold_in(arg_keys[4], part), 5)
    return {
        "traces": centred(part_keys[0], (2, ORDER, ORDER), 1.0, 6.0, ((1, 4), (2, 4))),
        "recv_live": set_ends((jax.random.randint(part_keys[1], (ORDER,), 0, 8) < 7).astype(jnp.int32), jax.random.fold_in(part_keys[1], 1), 0, 1),
        "missing": draw_missing(jax.random.fold_in(jax.random.fold_in(arg_keys[4], part), 71), part),
        "wavelet": jnp.clip(jax.random.uniform(part_keys[3], (2,), jnp.float32, 0.5, 1.5), 0.5, 1.5),
    }


def reference(traces, recv_live, missing, wavelet):
    tile_size = ORDER // N_ROW
    positions = jnp.arange(tile_size, dtype=jnp.int32)
    dead_rows = jnp.any(positions[None, :, None] == missing[:, None, :], axis=2).reshape(ORDER)
    shot_live = jnp.logical_not(dead_rows)
    recv_mask = recv_live == 1
    zero_bf = jnp.zeros((), jnp.bfloat16)
    direct = jnp.where(recv_mask[None, None, :], traces, zero_bf)
    flipped = jnp.swapaxes(traces, 1, 2)
    mirrored = jnp.where(recv_mask[None, :, None] & shot_live[None, None, :], flipped, zero_bf)
    filled = jnp.where(shot_live[None, :, None], direct, mirrored).astype(jnp.bfloat16)
    window = filled.reshape(2, ORDER, N_ROW, tile_size)[:, :, :, :WIN].reshape(2, ORDER, N_ROW * WIN)
    left_tile = filled.astype(jnp.float32)
    right_tile = window.astype(jnp.float32)

    def matmul(first, second):
        return jnp.dot(first, second, precision=lax.Precision.HIGHEST, preferred_element_type=jnp.float32)
    real_part = matmul(left_tile[0], right_tile[0]) - matmul(left_tile[1], right_tile[1])
    imag_part = matmul(left_tile[0], right_tile[1]) + matmul(left_tile[1], right_tile[0])
    norm_scale = 1.0 / math.sqrt(ORDER)
    pred_real = (wavelet[0] * real_part - wavelet[1] * imag_part) * norm_scale
    pred_imag = (wavelet[0] * imag_part + wavelet[1] * real_part) * norm_scale
    return jnp.stack([right_tile[0] - pred_real, right_tile[1] - pred_imag])
```

```python
import functools
import math

import jax
import jax.numpy as jnp
from jax import lax
from jax.experimental import pallas as pl
from jax.experimental.pallas import tpu as pltpu
from jax.sharding import PartitionSpec as P

F32 = jnp.float32
BF16 = jnp.bfloat16


def dot(first, second, dims=((1,), (0,)), **kw):
    return lax.dot_general(first, second, (dims, ((), ())), preferred_element_type=F32, **kw)


def make_local(order):
    def local(traces, recv_live, missing, wavelet):
        tile = traces.shape[1]
        grid = lax.axis_size("row")
        win = 128
        row = lax.axis_index("row")
        col = lax.axis_index("col")
        positions = jnp.arange(tile, dtype=jnp.int32)
        raw = traces[:, :, :win]
        gathered = lax.all_gather(raw, "row", axis=0, tiled=False)

        miss_row = lax.dynamic_index_in_dim(missing, row, 0, keepdims=False)
        miss_col = lax.dynamic_index_in_dim(missing, col, 0, keepdims=False)
        hot_row = positions[None, :] == miss_row[:, None]
        hot_col = positions[None, :] == miss_col[:, None]
        dead_row = jnp.any(hot_row, axis=0)
        dead_col = jnp.any(hot_col, axis=0)
        dead_win = jnp.any(missing[:, :, None] == positions[None, None, :win], axis=1)
        recv = (recv_live == 1).reshape(grid, tile)
        recv_row = lax.dynamic_index_in_dim(recv, row, 0, keepdims=False)
        recv_col = lax.dynamic_index_in_dim(recv, col, 0, keepdims=False)
        recv_miss_row = jnp.any(hot_row & recv_row[None, :], axis=1)
        recv_miss_col = jnp.any(hot_col & recv_col[None, :], axis=1)
        hot_row_b = hot_row.astype(BF16)
        hot_col_b = hot_col.astype(BF16)
        zero = jnp.zeros((), BF16)

        outgoing = jnp.stack([dot(hot_col_b, traces[p], ((1,), (1,))) for p in range(2)]).astype(BF16)
        route = [(r * grid + c, c * grid + r) for r in range(grid) for c in range(grid)]
        incoming = lax.ppermute(outgoing, ("row", "col"), route)
        dead_gather = lax.all_gather(outgoing[:, :, :win], "row", axis=0, tiled=False)

        swapped = lax.all_to_all(gathered, "col", split_axis=0, concat_axis=0, tiled=True)
        wide = jnp.transpose(swapped, (1, 2, 0, 3)).reshape(2, tile, grid * win)
        live_win = recv[:, :win].reshape(-1)
        keep = jnp.where(live_win[None, :] & ~dead_col[:, None], True, False)
        deads = jnp.transpose(dead_gather, (1, 2, 0, 3)).reshape(2, -1, grid * win)
        dead_keep = recv_miss_col[:, None] & ~dead_win.reshape(-1)[None, :]
        deads = jnp.where(dead_keep[None], deads, zero)
        window = [
            jnp.where(keep, wide[p], dot(hot_col_b, deads[p], ((0,), (0,))).astype(BF16))
            for p in range(2)
        ]
        masked = [jnp.where(recv_col[:, None], w, zero) for w in window]
        patched = jnp.where(recv_miss_row[None, :, None] & ~dead_col[None, None, :], incoming, zero)

        def product(left, right):
            first = jnp.concatenate([right[0], right[1]], axis=1)
            second = jnp.concatenate([-right[1], right[0]], axis=1)
            return dot(left[0], first) + dot(left[1], second)

        live = product(traces, masked)
        lost = product(patched, window)
        lost = dot(hot_row.astype(F32), lost, ((0,), (0,)), precision=lax.Precision.HIGHEST)
        partial = jnp.where(dead_row[:, None], lost, live)
        partial = jnp.transpose(partial.reshape(tile, 2, grid, win), (2, 1, 0, 3))
        total = lax.psum_scatter(partial, "col", scatter_dimension=0, tiled=True)[0]
        scale = 1.0 / math.sqrt(order)
        real = (wavelet[0] * total[0] - wavelet[1] * total[1]) * scale
        imag = (wavelet[0] * total[1] + wavelet[1] * total[0]) * scale
        own_in = lax.dynamic_index_in_dim(recv[:, :win], col, 0, keepdims=False)
        own_dead = jnp.where(
            recv_miss_row[None, :, None] & ~dead_col[None, None, :win], incoming[:, :, :win], zero
        )
        own = [
            jnp.where(
                dead_row[:, None],
                dot(hot_row_b, own_dead[p], ((0,), (0,))),
                jnp.where(own_in[None, :], raw[p], zero).astype(F32),
            )
            for p in range(2)
        ]
        return jnp.stack([own[0] - real, own[1] - imag])

    return local


MESH = pl.DeviceIdType.MESH
PIECES = 6
LANE = 4
CHUNKS = 3


def nt(first, second):
    return lax.dot_general(first, second, (((1,), (1,)), ((), ())), preferred_element_type=F32)


def mm(first, second):
    return jnp.dot(first, second, preferred_element_type=F32)


def fused_kernel(
    order, traces, recv, miss, miss_t, wavelet, out,
    tile_ref, ws, wown, wlive, wbuf, tbuf, psend, precv, part, sib, qsend, qrecv, ssend, srecv,
    xt, lost, up_in, down_in, hot_row, dead_ref, recv_rows,
    tile_sem, pat_s, pat_r, x_s, x_r, w_r, t_r, own_s, hub_s, fwd_s, tran_s,
    up_s, up_r, down_s, down_r, sib_s, sib_r, q_s, q_r, sc_s, sc_r,
):
    f = lax.axis_index("freq")
    r = lax.axis_index("row")
    c = lax.axis_index("col")
    grid = 4
    tile, win = tile_ref.shape[1], wown.shape[2]
    dead_n = xt.shape[2]
    rows = tile // PIECES
    extra = PIECES - LANE
    chunk = tile // CHUNKS
    rh, ch = r // 2, c // 2
    same = rh == ch
    hub = r == c
    inner = (r == 1) | (r == 2)
    r1 = r + 1 - 2 * (r % 2)
    c1 = c + 1 - 2 * (c % 2)
    cx = (c + 2) % 4
    mid_of_r = 2 - rh
    near_edge = 3 * rh
    far0 = 2 * (1 - ch)
    own0 = 2 * ch

    def sub(p):
        return pl.ds(pl.multiple_of(p * rows, rows), rows)

    def big(j):
        return pl.ds(pl.multiple_of(j * chunk, chunk), chunk)

    def rc(src, dst, ssem, rsem, dev):
        return pltpu.make_async_remote_copy(
            src_ref=src, dst_ref=dst, send_sem=ssem, recv_sem=rsem,
            device_id=(f, dev[0], dev[1]), device_id_type=MESH,
        )

    def own_copy(p, which):
        dev = [(r, r), (r1, r), (mid_of_r, r)][which]
        return rc(ws.at[:, sub(p)], wbuf.at[c, :, sub(p)], own_s.at[which, p], w_r.at[c, p], dev)

    def lane_copy(p, which):
        dev = [None, (r1, c), (mid_of_r, c)][which]
        slot = r % 2
        return rc(ws.at[:, sub(p)], tbuf.at[slot, :, sub(p)], own_s.at[which, p], t_r.at[slot, p], dev)

    def hub_copy(i, e, which):
        b, p = far0 + i, LANE + e
        dev = [(r1, r), (mid_of_r, r)][which]
        return rc(wbuf.at[b, :, sub(p)], wbuf.at[b, :, sub(p)], hub_s.at[i, e, which], w_r.at[b, p], dev)

    def fwd_copy(b, p):
        return rc(wbuf.at[b, :, sub(p)], wbuf.at[b, :, sub(p)], fwd_s.at[b, p], w_r.at[b, p], (near_edge, c))

    def cross_copy(k, p):
        slot = k % 2
        return rc(tbuf.at[slot, :, sub(p)], wbuf.at[c, :, sub(p)], tran_s.at[slot, p, 0], w_r.at[c, p], (r, k))

    def pass_copy(k, p):
        slot = k % 2
        return rc(tbuf.at[slot, :, sub(p)], tbuf.at[slot, :, sub(p)], tran_s.at[slot, p, 1], t_r.at[slot, p], (near_edge, c))

    def wait_w(b, p):
        rc(wbuf.at[b, :, sub(p)], wbuf.at[b, :, sub(p)], fwd_s.at[b, p], w_r.at[b, p], (r, c1)).wait_recv()

    def wait_t(slot, p):
        rc(tbuf.at[slot, :, sub(p)], tbuf.at[slot, :, sub(p)], tran_s.at[slot, p, 0], t_r.at[slot, p], (r, c1)).wait_recv()

    def x_copy(which):
        src = [c, c, cx][which]
        dev = [(r, c1), (r, cx), (r, c1)][which]
        return rc(xt.at[src], xt.at[src], x_s.at[which], x_r.at[src], dev)

    def wait_x(b):
        rc(xt.at[b], xt.at[b], x_s.at[0], x_r.at[b], (r, c1)).wait_recv()

    def up_copy(b):
        return rc(lost.at[0, b], up_in.at[b], up_s.at[b], up_r.at[b], (jnp.minimum(r + 1, grid - 1), c))

    def down_copy(b):
        return rc(lost.at[1, b], down_in.at[b], down_s.at[b], down_r.at[b], (jnp.maximum(r - 1, 0), c))

    def sib_copy(phase, b, j):
        return rc(part.at[b, big(j)], sib.at[phase, big(j)], sib_s.at[phase, j], sib_r.at[phase, j], (r, c1))

    def q_copy(j):
        return rc(qsend.at[big(j)], qrecv.at[big(j)], q_s.at[j], q_r.at[j], (r, cx))

    def sc_copy(j):
        return rc(ssend.at[j], srecv.at[j], sc_s.at[j], sc_r.at[j], (r, cx))

    pat = rc(psend, precv, pat_s.at[0], pat_r.at[0], (c, r))

    head = pltpu.make_async_copy(traces.at[:, pl.ds(0, win)], tile_ref.at[:, pl.ds(0, win)], tile_sem.at[0])
    rest = pltpu.make_async_copy(
        traces.at[:, pl.ds(win, tile - win)], tile_ref.at[:, pl.ds(win, tile - win)], tile_sem.at[1])
    head.start()
    rest.start()
    barrier = pltpu.get_barrier_semaphore()
    for n in range(1, grid * grid):
        other = (r * grid + c + n) % (grid * grid)
        pl.semaphore_signal(
            barrier, inc=1, device_id=(f, other // grid, other % grid), device_id_type=MESH)

    recv_c = recv[pl.ds(c, 1), :]
    recv_r = recv[pl.ds(r, 1), :]
    pick = lax.broadcasted_iota(jnp.int32, miss_t.shape, 1)
    miss_c = jnp.sum(jnp.where(pick == c, miss_t[...], 0), axis=1, keepdims=True)
    miss_r = jnp.sum(jnp.where(pick == r, miss_t[...], 0), axis=1, keepdims=True)
    place = lax.broadcasted_iota(jnp.int32, (dead_n, tile), 1)
    hot_col = jnp.where((place == miss_c) & (recv_c == 1), 1.0, 0.0).astype(BF16)
    head_hot = jnp.where(place[:, :win] == miss_r, 1.0, 0.0)
    live_q = 1.0 - jnp.max(head_hot, axis=0, keepdims=True)
    recv_q = jnp.where(recv_c[:, :win] == 1, 1.0, 0.0)
    miss_row = miss[pl.ds(r, 1), :]
    ones = jnp.ones((dead_n, win), BF16)
    for j in range(CHUNKS):
        spot = lax.broadcasted_iota(jnp.int32, (chunk, dead_n), 0) + j * chunk
        hot = jnp.where(spot == miss_row, 1.0, 0.0).astype(BF16)
        hot_row[pl.ds(j * chunk, chunk), :] = hot
        dead_ref[pl.ds(j * chunk, chunk), :] = mm(hot, ones)
    for j in range(tile // win):
        lane = jnp.where(recv_r[:, j * win:(j + 1) * win] == 1, 1.0, 0.0)
        recv_rows[pl.ds(j * win, win), :] = jnp.transpose(jnp.broadcast_to(lane, (win, win)))

    head.wait()
    for p in range(2):
        psend[p] = (nt(hot_col, tile_ref[p, :win, :]) * live_q).astype(BF16)
    pl.semaphore_wait(barrier, grid * grid - 1)

    @pl.when(hub)
    def _():
        precv[...] = psend[...]

    @pl.when(jnp.logical_not(hub))
    def _():
        pat.start()

    rest.wait()
    for p in range(2):
        for j in range(CHUNKS):
            xt[c, p, :, pl.ds(j * chunk, chunk)] = nt(hot_col, tile_ref[p, pl.ds(j * chunk, chunk), :]).astype(BF16)
    x_copy(0).start()
    x_copy(1).start()

    for p in range(2):
        for j in range(CHUNKS):
            s = pl.ds(j * chunk, chunk)
            raw = tile_ref[p, s, :win].astype(F32) * recv_q
            wlive[p, s] = jnp.where(dead_ref[s] > 0.5, 0.0, raw).astype(BF16)

    @pl.when(jnp.logical_not(hub))
    def _():
        pat.wait_recv()

    for p in range(2):
        for j in range(CHUNKS):
            s = pl.ds(j * chunk, chunk)
            full = wlive[p, s].astype(F32) + mm(hot_row[s], precv[p])
            wown[p, s] = full.astype(BF16)
            ws[p, s] = (full * recv_rows[s]).astype(BF16)

    @pl.when(hub)
    def _():
        wbuf[c] = ws[...]

    @pl.when(same & jnp.logical_not(hub))
    def _():
        @pl.loop(0, PIECES)
        def _(p):
            own_copy(p, 2).start()
            own_copy(p, 1).start()
            own_copy(p, 0).start()

    @pl.when(jnp.logical_not(same))
    def _():
        @pl.loop(LANE, PIECES)
        def _(p):
            own_copy(p, 0).start()

        @pl.loop(0, LANE)
        def _(p):
            lane_copy(p, 2).start()
            lane_copy(p, 1).start()
            own_copy(p, 0).start()

    zero = jnp.zeros((chunk, 2 * win), F32)
    for b in range(grid):
        for j in range(CHUNKS):
            part[b, pl.ds(j * chunk, chunk)] = zero

    def accumulate(b, p):
        k = sub(p)
        re, im = wbuf[b, 0, k, :], wbuf[b, 1, k, :]
        first = jnp.concatenate([re, im], axis=1)
        second = jnp.concatenate([-im, re], axis=1)

        @pl.loop(0, CHUNKS)
        def _(j):
            s = big(j)
            part[b, s] += mm(tile_ref[0, s, k], first) + mm(tile_ref[1, s, k], second)

    def take_near(p, blocks=(c1, c)):
        for b in blocks:
            @pl.when(jnp.logical_not((inner & jnp.logical_not(same)) | (hub & (b == c))))
            def _():
                wait_w(b, p)
            accumulate(b, p)

    def forward_near(p):
        @pl.when(hub)
        def _():
            own_copy(p, 2).start()
            own_copy(p, 1).start()

        @pl.when(inner & jnp.logical_not(same))
        def _():
            for i in range(2):
                wait_w(own0 + i, p)
                fwd_copy(own0 + i, p).start()

    @pl.loop(0, LANE)
    def _(p):
        @pl.when(same)
        def _():
            for i in range(2):
                k = far0 + i
                wait_t(i, p)

                @pl.when(inner)
                def _():
                    pass_copy(k, p).start()
                cross_copy(k, p).start()

        @pl.when(jnp.logical_not(same))
        def _():
            wait_t(r1 % 2, p)
            cross_copy(r1, p).start()

        @pl.when(hub & (p < extra))
        def _():
            for i in range(2):
                wait_w(far0 + i, LANE + p)
                for which in range(2):
                    hub_copy(i, p, which).start()

        @pl.when(inner & jnp.logical_not(same) & (p >= 1) & (p <= extra))
        def _():
            for i in range(2):
                wait_w(far0 + i, LANE + p - 1)
                fwd_copy(far0 + i, LANE + p - 1).start()
        forward_near(p)

        @pl.when(p >= 1)
        def _():
            for i in range(2):
                wait_w(far0 + i, p - 1)
                accumulate(far0 + i, p - 1)
            take_near(p - 1)

    wait_x(cx)
    x_copy(2).start()
    re, im = wlive[0], wlive[1]
    first = jnp.concatenate([re, im], axis=1)
    second = jnp.concatenate([-im, re], axis=1)
    wait_x(c1)
    wait_x((c1 + 2) % 4)
    for b in range(grid):
        value = mm(xt[b, 0], first) + mm(xt[b, 1], second)
        lost[0, b] = value
        lost[1, b] = value * jnp.where(r == b, 0.0, 1.0)
    for b in range(1, grid):
        @pl.when((r == 0))
        def _():
            up_copy(b).start()

        @pl.when((r == grid - 1))
        def _():
            down_copy(grid - 1 - b).start()

    forward_near(LANE)

    def take_far(i):
        b = far0 + i
        wait_w(b, LANE - 1)
        accumulate(b, LANE - 1)
        for e in range(extra):
            @pl.when(jnp.logical_not(hub | (inner & jnp.logical_not(same))))
            def _():
                wait_w(b, LANE + e)
            accumulate(b, LANE + e)

    side = c % 2
    take_far(1 - side)
    for j in range(CHUNKS):
        sib_copy(0, far0 + 1 - side, j).start()
    take_far(side)
    for j in range(CHUNKS):
        s = big(j)
        sib_copy(0, far0 + 1 - side, j).wait_recv()
        value = part[far0 + side, s] + sib[0, s]
        top = jnp.max(jnp.abs(value), axis=0, keepdims=True)
        ratio = jnp.where(top > 0.0, 32767.0 / jnp.maximum(top, 1e-30), 0.0)
        qsend[s] = jnp.round(value * ratio).astype(jnp.int32).astype(jnp.int16)
        ssend[j] = jnp.broadcast_to(top * (1.0 / 32767.0), ssend.shape[1:])
        q_copy(j).start()
        sc_copy(j).start()

    def hop(step):
        @pl.when(r == step)
        def _():
            for b in range(step, grid):
                up_copy(b).wait_recv()
            for b in range(step, grid):
                lost[0, b] = lost[0, b] + up_in[b]
            for b in range(step + 1, grid):
                up_copy(b).start()

        @pl.when(r == grid - 1 - step)
        def _():
            for b in range(0, grid - step):
                down_copy(b).wait_recv()
            for b in range(0, grid - step):
                lost[1, b] = lost[1, b] + down_in[b]
            for b in range(0, grid - 1 - step):
                down_copy(b).start()

    hop(1)
    take_near(LANE - 1)
    hop(2)
    for p in range(LANE, PIECES):
        if p > LANE:
            forward_near(p)
        if p < PIECES - 1:
            take_near(p)
    hop(3)
    take_near(PIECES - 1, (c1,))
    for j in range(CHUNKS):
        sib_copy(1, c1, j).start()
    take_near(PIECES - 1, (c,))

    value = lost[0, r] + lost[1, r]
    part_hi = value.astype(BF16)
    left = value - part_hi.astype(F32)
    part_mid = left.astype(BF16)
    part_lo = (left - part_mid.astype(F32)).astype(BF16)
    scale = 1.0 / math.sqrt(order)
    w0, w1 = wavelet[0] * scale, wavelet[1] * scale
    for j in range(CHUNKS):
        s = big(j)
        spread = mm(hot_row[s], part_hi) + mm(hot_row[s], part_mid) + mm(hot_row[s], part_lo)
        q_copy(j).wait_recv()
        sc_copy(j).wait_recv()
        sib_copy(1, c1, j).wait_recv()
        total = part[c, s] + sib[1, s] + qrecv[s].astype(jnp.int32).astype(F32) * srecv[j, 0:1, :]
        dead = dead_ref[s] > 0.5
        real = jnp.where(dead, spread[:, :win], total[:, :win])
        imag = jnp.where(dead, spread[:, win:], total[:, win:])
        out[0, s] = wown[0, s].astype(F32) - (w0 * real - w1 * imag)
        out[1, s] = wown[1, s].astype(F32) - (w0 * imag + w1 * real)

    x_copy(0).wait_send()
    x_copy(1).wait_send()
    x_copy(2).wait_send()
    for j in range(CHUNKS):
        sib_copy(0, far0 + 1 - side, j).wait_send()
        sib_copy(1, c1, j).wait_send()
        q_copy(j).wait_send()
        sc_copy(j).wait_send()
    for b in range(grid):
        @pl.when((b > r) & (r < grid - 1))
        def _():
            up_copy(b).wait_send()

        @pl.when((b < r) & (r > 0))
        def _():
            down_copy(b).wait_send()

    @pl.when(jnp.logical_not(hub))
    def _():
        pat.wait_send()

    @pl.when(same)
    def _():
        @pl.loop(0, PIECES)
        def _(p):
            own_copy(p, 2).wait_send()
            own_copy(p, 1).wait_send()

            @pl.when(jnp.logical_not(hub))
            def _():
                own_copy(p, 0).wait_send()

        @pl.loop(0, LANE)
        def _(p):
            for i in range(2):
                cross_copy(far0 + i, p).wait_send()

                @pl.when(inner)
                def _():
                    pass_copy(far0 + i, p).wait_send()

    @pl.when(hub)
    def _():
        for i in range(2):
            for e in range(extra):
                for which in range(2):
                    hub_copy(i, e, which).wait_send()

    @pl.when(jnp.logical_not(same))
    def _():
        @pl.loop(0, PIECES)
        def _(p):
            own_copy(p, 0).wait_send()

        @pl.loop(0, LANE)
        def _(p):
            lane_copy(p, 2).wait_send()
            lane_copy(p, 1).wait_send()
            cross_copy(r1, p).wait_send()

        @pl.when(inner)
        def _():
            @pl.loop(0, PIECES)
            def _(p):
                for i in range(2):
                    fwd_copy(own0 + i, p).wait_send()
            for i in range(2):
                for e in range(extra):
                    fwd_copy(far0 + i, LANE + e).wait_send()


def make_fused(order):
    def local(traces, recv_live, missing, wavelet):
        tile = traces.shape[1]
        grid, dead_n = missing.shape
        win = 128
        recv = recv_live.reshape(grid, tile)
        dma, vmem = pltpu.SemaphoreType.DMA, pltpu.VMEM
        block = (2, tile, win)
        wide = (tile, 2 * win)
        scratch = [
            vmem((2, tile, tile), BF16),
            vmem(block, BF16), vmem(block, BF16), vmem(block, BF16),
            vmem((grid,) + block, BF16), vmem((2,) + block, BF16),
            vmem((2, dead_n, win), BF16), vmem((2, dead_n, win), BF16),
            vmem((grid,) + wide, F32), vmem((2,) + wide, F32),
            vmem(wide, jnp.int16), vmem(wide, jnp.int16),
            vmem((CHUNKS, 8, 2 * win), F32), vmem((CHUNKS, 8, 2 * win), F32),
            vmem((grid, 2, dead_n, tile), BF16),
            vmem((2, grid, dead_n, 2 * win), F32),
            vmem((grid, dead_n, 2 * win), F32), vmem((grid, dead_n, 2 * win), F32),
            vmem((tile, dead_n), BF16), vmem((tile, win), F32), vmem((tile, win), F32),
            dma((2,)), dma((1,)), dma((1,)), dma((3,)), dma((grid,)),
            dma((grid, PIECES)), dma((2, LANE)), dma((3, PIECES)), dma((2, PIECES - LANE, 2)),
            dma((grid, PIECES)), dma((2, LANE, 2)),
            dma((grid,)), dma((grid,)), dma((grid,)), dma((grid,)),
            dma((2, CHUNKS)), dma((2, CHUNKS)),
            dma((CHUNKS,)), dma((CHUNKS,)), dma((CHUNKS,)), dma((CHUNKS,)),
        ]
        whole = pl.BlockSpec(memory_space=pltpu.VMEM)
        return pl.pallas_call(
            functools.partial(fused_kernel, order),
            out_shape=jax.ShapeDtypeStruct(block, F32),
            in_specs=[
                pl.BlockSpec(memory_space=pl.ANY), whole, whole, whole,
                pl.BlockSpec(memory_space=pltpu.SMEM),
            ],
            out_specs=whole,
            scratch_shapes=scratch,
            compiler_params=pltpu.CompilerParams(
                collective_id=0, has_side_effects=True, vmem_limit_bytes=56 * 2**20
            ),
        )(traces, recv, missing, missing.T, wavelet)

    return local


def solution(mesh):
    in_specs = (P("freq", "row", "col"), P("freq"), P("freq", None), P("freq"))
    out_specs = P("freq", "row", "col")
    small = mesh.shape["row"] == 4 and mesh.shape["col"] == 4

    def run(traces, recv_live, missing, wavelet):
        local = (make_fused if small else make_local)(traces.shape[1])
        return jax.shard_map(
            local, mesh=mesh, in_specs=in_specs, out_specs=out_specs, check_vma=False
        )(traces, recv_live, missing, wavelet)

    return run
```

```python
import functools
import math

import jax
import jax.numpy as jnp
from jax import lax
from jax.experimental import pallas as pl
from jax.experimental.pallas import tpu as pltpu
from jax.sharding import PartitionSpec as P

F32 = jnp.float32
BF16 = jnp.bfloat16


def dot(first, second, dims=((1,), (0,)), **kw):
    return lax.dot_general(first, second, (dims, ((), ())), preferred_element_type=F32, **kw)


def make_local(order):
    def local(traces, recv_live, missing, wavelet):
        tile = traces.shape[1]
        grid = lax.axis_size("row")
        win = 128
        row = lax.axis_index("row")
        col = lax.axis_index("col")
        positions = jnp.arange(tile, dtype=jnp.int32)
        raw = traces[:, :, :win]
        gathered = lax.all_gather(raw, "row", axis=0, tiled=False)

        miss_row = lax.dynamic_index_in_dim(missing, row, 0, keepdims=False)
        miss_col = lax.dynamic_index_in_dim(missing, col, 0, keepdims=False)
        hot_row = positions[None, :] == miss_row[:, None]
        hot_col = positions[None, :] == miss_col[:, None]
        dead_row = jnp.any(hot_row, axis=0)
        dead_col = jnp.any(hot_col, axis=0)
        dead_win = jnp.any(missing[:, :, None] == positions[None, None, :win], axis=1)
        recv = (recv_live == 1).reshape(grid, tile)
        recv_row = lax.dynamic_index_in_dim(recv, row, 0, keepdims=False)
        recv_col = lax.dynamic_index_in_dim(recv, col, 0, keepdims=False)
        recv_miss_row = jnp.any(hot_row & recv_row[None, :], axis=1)
        recv_miss_col = jnp.any(hot_col & recv_col[None, :], axis=1)
        hot_row_b = hot_row.astype(BF16)
        hot_col_b = hot_col.astype(BF16)
        zero = jnp.zeros((), BF16)

        outgoing = jnp.stack([dot(hot_col_b, traces[p], ((1,), (1,))) for p in range(2)]).astype(BF16)
        route = [(r * grid + c, c * grid + r) for r in range(grid) for c in range(grid)]
        incoming = lax.ppermute(outgoing, ("row", "col"), route)
        dead_gather = lax.all_gather(outgoing[:, :, :win], "row", axis=0, tiled=False)

        swapped = lax.all_to_all(gathered, "col", split_axis=0, concat_axis=0, tiled=True)
        wide = jnp.transpose(swapped, (1, 2, 0, 3)).reshape(2, tile, grid * win)
        live_win = recv[:, :win].reshape(-1)
        keep = jnp.where(live_win[None, :] & ~dead_col[:, None], True, False)
        deads = jnp.transpose(dead_gather, (1, 2, 0, 3)).reshape(2, -1, grid * win)
        dead_keep = recv_miss_col[:, None] & ~dead_win.reshape(-1)[None, :]
        deads = jnp.where(dead_keep[None], deads, zero)
        window = [
            jnp.where(keep, wide[p], dot(hot_col_b, deads[p], ((0,), (0,))).astype(BF16))
            for p in range(2)
        ]
        masked = [jnp.where(recv_col[:, None], w, zero) for w in window]
        patched = jnp.where(recv_miss_row[None, :, None] & ~dead_col[None, None, :], incoming, zero)

        def product(left, right):
            first = jnp.concatenate([right[0], right[1]], axis=1)
            second = jnp.concatenate([-right[1], right[0]], axis=1)
            return dot(left[0], first) + dot(left[1], second)

        live = product(traces, masked)
        lost = product(patched, window)
        lost = dot(hot_row.astype(F32), lost, ((0,), (0,)), precision=lax.Precision.HIGHEST)
        partial = jnp.where(dead_row[:, None], lost, live)
        partial = jnp.transpose(partial.reshape(tile, 2, grid, win), (2, 1, 0, 3))
        total = lax.psum_scatter(partial, "col", scatter_dimension=0, tiled=True)[0]
        scale = 1.0 / math.sqrt(order)
        real = (wavelet[0] * total[0] - wavelet[1] * total[1]) * scale
        imag = (wavelet[0] * total[1] + wavelet[1] * total[0]) * scale
        own_in = lax.dynamic_index_in_dim(recv[:, :win], col, 0, keepdims=False)
        own_dead = jnp.where(
            recv_miss_row[None, :, None] & ~dead_col[None, None, :win], incoming[:, :, :win], zero
        )
        own = [
            jnp.where(
                dead_row[:, None],
                dot(hot_row_b, own_dead[p], ((0,), (0,))),
                jnp.where(own_in[None, :], raw[p], zero).astype(F32),
            )
            for p in range(2)
        ]
        return jnp.stack([own[0] - real, own[1] - imag])

    return local


MESH = pl.DeviceIdType.MESH
PIECES = 6
LANE = 4
CHUNKS = 3


def nt(first, second):
    return lax.dot_general(first, second, (((1,), (1,)), ((), ())), preferred_element_type=F32)


def mm(first, second):
    return jnp.dot(first, second, preferred_element_type=F32)


def fused_kernel(
    order, traces, recv, miss, miss_t, wavelet, out,
    tile_ref, ws, wown, wlive, wbuf, tbuf, psend, precv, part, sib, qsend, qrecv, ssend, srecv,
    xt, lost, up_in, down_in, hot_row, dead_ref, recv_rows,
    tile_sem, pat_s, pat_r, x_s, x_r, w_r, t_r, own_s, hub_s, fwd_s, tran_s,
    up_s, up_r, down_s, down_r, sib_s, sib_r, q_s, q_r, sc_s, sc_r,
):
    f = lax.axis_index("freq")
    r = lax.axis_index("row")
    c = lax.axis_index("col")
    grid = 4
    tile, win = tile_ref.shape[1], wown.shape[2]
    dead_n = xt.shape[2]
    rows = tile // PIECES
    extra = PIECES - LANE
    chunk = tile // CHUNKS
    rh, ch = r // 2, c // 2
    same = rh == ch
    hub = r == c
    inner = (r == 1) | (r == 2)
    r1 = r + 1 - 2 * (r % 2)
    c1 = c + 1 - 2 * (c % 2)
    cx = (c + 2) % 4
    mid_of_r = 2 - rh
    near_edge = 3 * rh
    far0 = 2 * (1 - ch)
    own0 = 2 * ch

    def sub(p):
        return pl.ds(pl.multiple_of(p * rows, rows), rows)

    def big(j):
        return pl.ds(pl.multiple_of(j * chunk, chunk), chunk)

    def rc(src, dst, ssem, rsem, dev):
        return pltpu.make_async_remote_copy(
            src_ref=src, dst_ref=dst, send_sem=ssem, recv_sem=rsem,
            device_id=(f, dev[0], dev[1]), device_id_type=MESH,
        )

    def own_copy(p, which):
        dev = [(r, r), (r1, r), (mid_of_r, r)][which]
        return rc(ws.at[:, sub(p)], wbuf.at[c, :, sub(p)], own_s.at[which, p], w_r.at[c, p], dev)

    def lane_copy(p, which):
        dev = [None, (r1, c), (mid_of_r, c)][which]
        slot = r % 2
        return rc(ws.at[:, sub(p)], tbuf.at[slot, :, sub(p)], own_s.at[which, p], t_r.at[slot, p], dev)

    def hub_copy(i, e, which):
        b, p = far0 + i, LANE + e
        dev = [(r1, r), (mid_of_r, r)][which]
        return rc(wbuf.at[b, :, sub(p)], wbuf.at[b, :, sub(p)], hub_s.at[i, e, which], w_r.at[b, p], dev)

    def fwd_copy(b, p):
        return rc(wbuf.at[b, :, sub(p)], wbuf.at[b, :, sub(p)], fwd_s.at[b, p], w_r.at[b, p], (near_edge, c))

    def cross_copy(k, p):
        slot = k % 2
        return rc(tbuf.at[slot, :, sub(p)], wbuf.at[c, :, sub(p)], tran_s.at[slot, p, 0], w_r.at[c, p], (r, k))

    def pass_copy(k, p):
        slot = k % 2
        return rc(tbuf.at[slot, :, sub(p)], tbuf.at[slot, :, sub(p)], tran_s.at[slot, p, 1], t_r.at[slot, p], (near_edge, c))

    def wait_w(b, p):
        rc(wbuf.at[b, :, sub(p)], wbuf.at[b, :, sub(p)], fwd_s.at[b, p], w_r.at[b, p], (r, c1)).wait_recv()

    def wait_t(slot, p):
        rc(tbuf.at[slot, :, sub(p)], tbuf.at[slot, :, sub(p)], tran_s.at[slot, p, 0], t_r.at[slot, p], (r, c1)).wait_recv()

    def x_copy(which, p):
        src = [c, c, cx][which]
        dev = [(r, c1), (r, cx), (r, c1)][which]
        return rc(xt.at[src, p], xt.at[src, p], x_s.at[which, p], x_r.at[src, p], dev)

    def wait_x(b, p):
        rc(xt.at[b, p], xt.at[b, p], x_s.at[0, p], x_r.at[b, p], (r, c1)).wait_recv()

    def up_copy(b):
        return rc(lost.at[0, b], up_in.at[b], up_s.at[b], up_r.at[b], (jnp.minimum(r + 1, grid - 1), c))

    def down_copy(b):
        return rc(lost.at[1, b], down_in.at[b], down_s.at[b], down_r.at[b], (jnp.maximum(r - 1, 0), c))

    def sib_copy(phase, b, j):
        return rc(part.at[b, big(j)], sib.at[phase, big(j)], sib_s.at[phase, j], sib_r.at[phase, j], (r, c1))

    def q_copy(j):
        return rc(qsend.at[big(j)], qrecv.at[big(j)], q_s.at[j], q_r.at[j], (r, cx))

    def sc_copy(j):
        return rc(ssend.at[j], srecv.at[j], sc_s.at[j], sc_r.at[j], (r, cx))

    pat = rc(psend, precv, pat_s.at[0], pat_r.at[0], (c, r))

    head = pltpu.make_async_copy(traces.at[:, pl.ds(0, win)], tile_ref.at[:, pl.ds(0, win)], tile_sem.at[0])
    rest = pltpu.make_async_copy(
        traces.at[:, pl.ds(win, tile - win)], tile_ref.at[:, pl.ds(win, tile - win)], tile_sem.at[1])
    head.start()
    rest.start()
    barrier = pltpu.get_barrier_semaphore()
    for n in range(1, grid * grid):
        other = (r * grid + c + n) % (grid * grid)
        pl.semaphore_signal(
            barrier, inc=1, device_id=(f, other // grid, other % grid), device_id_type=MESH)

    recv_c = recv[pl.ds(c, 1), :]
    recv_r = recv[pl.ds(r, 1), :]
    pick = lax.broadcasted_iota(jnp.int32, miss_t.shape, 1)
    miss_c = jnp.sum(jnp.where(pick == c, miss_t[...], 0), axis=1, keepdims=True)
    miss_r = jnp.sum(jnp.where(pick == r, miss_t[...], 0), axis=1, keepdims=True)
    place = lax.broadcasted_iota(jnp.int32, (dead_n, tile), 1)
    hot_col = jnp.where((place == miss_c) & (recv_c == 1), 1.0, 0.0).astype(BF16)
    head_hot = jnp.where(place[:, :win] == miss_r, 1.0, 0.0)
    live_q = 1.0 - jnp.max(head_hot, axis=0, keepdims=True)
    recv_q = jnp.where(recv_c[:, :win] == 1, 1.0, 0.0)
    miss_row = miss[pl.ds(r, 1), :]
    ones = jnp.ones((dead_n, win), BF16)
    for j in range(CHUNKS):
        spot = lax.broadcasted_iota(jnp.int32, (chunk, dead_n), 0) + j * chunk
        hot = jnp.where(spot == miss_row, 1.0, 0.0).astype(BF16)
        hot_row[pl.ds(j * chunk, chunk), :] = hot
        dead_ref[pl.ds(j * chunk, chunk), :] = mm(hot, ones)
    for j in range(tile // win):
        lane = jnp.where(recv_r[:, j * win:(j + 1) * win] == 1, 1.0, 0.0)
        recv_rows[pl.ds(j * win, win), :] = jnp.transpose(jnp.broadcast_to(lane, (win, win)))

    head.wait()
    for p in range(2):
        psend[p] = (nt(hot_col, tile_ref[p, :win, :]) * live_q).astype(BF16)
    pl.semaphore_wait(barrier, grid * grid - 1)

    @pl.when(hub)
    def _():
        precv[...] = psend[...]

    @pl.when(jnp.logical_not(hub))
    def _():
        pat.start()

    rest.wait()
    for p in range(2):
        for j in range(CHUNKS):
            xt[c, p, :, pl.ds(j * chunk, chunk)] = nt(hot_col, tile_ref[p, pl.ds(j * chunk, chunk), :]).astype(BF16)
    for p in range(2):
        for j in range(CHUNKS):
            s = pl.ds(j * chunk, chunk)
            raw = tile_ref[p, s, :win].astype(F32) * recv_q
            wlive[p, s] = jnp.where(dead_ref[s] > 0.5, 0.0, raw).astype(BF16)

    @pl.when(jnp.logical_not(hub))
    def _():
        pat.wait_recv()

    for p in range(2):
        for j in range(CHUNKS):
            s = pl.ds(j * chunk, chunk)
            full = wlive[p, s].astype(F32) + mm(hot_row[s], precv[p])
            wown[p, s] = full.astype(BF16)
            ws[p, s] = (full * recv_rows[s]).astype(BF16)

    @pl.when(hub)
    def _():
        wbuf[c] = ws[...]

    @pl.when(same & jnp.logical_not(hub))
    def _():
        @pl.loop(0, PIECES)
        def _(p):
            own_copy(p, 2).start()
            own_copy(p, 1).start()
            own_copy(p, 0).start()

    @pl.when(jnp.logical_not(same))
    def _():
        @pl.loop(LANE, PIECES)
        def _(p):
            own_copy(p, 0).start()

        @pl.loop(0, LANE)
        def _(p):
            lane_copy(p, 2).start()
            lane_copy(p, 1).start()
            own_copy(p, 0).start()

    x_copy(1, 0).start()
    x_copy(1, 1).start()

    @pl.when(hub)
    def _():
        own_copy(0, 2).start()
        own_copy(0, 1).start()
        for e in range(extra):
            for i in range(2):
                wait_w(far0 + i, LANE + e)
                for which in range(2):
                    hub_copy(i, e, which).start()

        @pl.loop(1, PIECES)
        def _(p):
            own_copy(p, 2).start()
            own_copy(p, 1).start()
    x_copy(0, 0).start()
    x_copy(0, 1).start()

    relay = inner & jnp.logical_not(same)

    def accumulate(b, p, count, fresh=False):
        k = pl.ds(pl.multiple_of(p * rows, rows), count * rows)
        re, im = wbuf[b, 0, k, :], wbuf[b, 1, k, :]
        first = jnp.concatenate([re, im], axis=1)
        second = jnp.concatenate([-im, re], axis=1)

        @pl.loop(0, CHUNKS)
        def _(j):
            s = big(j)
            value = mm(tile_ref[0, s, k], first) + mm(tile_ref[1, s, k], second)
            part[b, s] = value if fresh else part[b, s] + value

    def relay_piece(b, p):
        @pl.when(relay)
        def _():
            wait_w(b, p)
            fwd_copy(b, p).start()

    def transit(p):
        @pl.when(same)
        def _():
            for i in range(2):
                k = far0 + i
                wait_t(i, p)

                @pl.when(inner)
                def _():
                    pass_copy(k, p).start()
                cross_copy(k, p).start()

        @pl.when(jnp.logical_not(same))
        def _():
            wait_t(r1 % 2, p)
            cross_copy(r1, p).start()

    def take_far(b, p, count, fresh=False):
        for n in range(count):
            if p + n < LANE:
                wait_w(b, p + n)
            else:
                @pl.when(jnp.logical_not(hub | relay))
                def _():
                    wait_w(b, p + n)
        accumulate(b, p, count, fresh)

    def take_near(b, p, count, fresh=False):
        for n in range(count):
            @pl.when(jnp.logical_not(relay | (hub & (b == c))))
            def _():
                wait_w(b, p + n)
        accumulate(b, p, count, fresh)

    def hop(step):
        @pl.when(r == step)
        def _():
            for b in range(step, grid):
                up_copy(b).wait_recv()
            for b in range(step, grid):
                lost[0, b] = lost[0, b] + up_in[b]
            for b in range(step + 1, grid):
                up_copy(b).start()

        @pl.when(r == grid - 1 - step)
        def _():
            for b in range(0, grid - step):
                down_copy(b).wait_recv()
            for b in range(0, grid - step):
                lost[1, b] = lost[1, b] + down_in[b]
            for b in range(0, grid - 1 - step):
                down_copy(b).start()

    side = c % 2
    far_own, far_sib = far0 + side, far0 + 1 - side
    hub_order = [(c, 0)] + [(far0 + i, LANE + e) for e in range(extra) for i in range(2)] + [(c, p) for p in range(1, PIECES)]

    def near_relays(first, last):
        for t in range(first, last):
            if t < PIECES:
                relay_piece(c1, t)
            relay_piece(*hub_order[t])

    transit(0)
    near_relays(0, 1)
    transit(1)
    near_relays(1, 2)
    transit(2)
    near_relays(2, 3)
    take_far(far_sib, 0, 2, True)
    take_far(far_own, 0, 2, True)
    transit(3)
    near_relays(3, 4)

    for p in range(2):
        wait_x(cx, p)
        x_copy(2, p).start()
    take_far(far_sib, 2, 2)
    take_far(far_own, 2, 2)
    near_relays(4, 5)
    re, im = wlive[0], wlive[1]
    first = jnp.concatenate([re, im], axis=1)
    second = jnp.concatenate([-im, re], axis=1)
    for p in range(2):
        wait_x(c1, p)
        wait_x((c1 + 2) % 4, p)
    for b in range(grid):
        value = mm(xt[b, 0], first) + mm(xt[b, 1], second)
        lost[0, b] = value
        lost[1, b] = value * jnp.where(r == b, 0.0, 1.0)
    for b in range(1, grid):
        @pl.when((r == 0))
        def _():
            up_copy(b).start()

        @pl.when((r == grid - 1))
        def _():
            down_copy(grid - 1 - b).start()

    take_far(far_sib, LANE, extra)
    for j in range(CHUNKS):
        sib_copy(0, far_sib, j).start()
    take_far(far_own, LANE, extra)
    for j in range(CHUNKS):
        s = big(j)
        sib_copy(0, far_sib, j).wait_recv()
        value = part[far_own, s] + sib[0, s]
        top = jnp.max(jnp.abs(value), axis=0, keepdims=True)
        ratio = jnp.where(top > 0.0, 32767.0 / jnp.maximum(top, 1e-30), 0.0)
        qsend[s] = jnp.round(value * ratio).astype(jnp.int32).astype(jnp.int16)
        ssend[j] = jnp.broadcast_to(top * (1.0 / 32767.0), ssend.shape[1:])
        q_copy(j).start()
        sc_copy(j).start()
    near_relays(5, 6)
    take_near(c1, 0, 3, True)
    near_relays(6, 7)
    hop(1)
    take_near(c1, 3, 3)
    for j in range(CHUNKS):
        sib_copy(1, c1, j).start()
    near_relays(7, 8)
    take_near(c, 0, 2, True)
    near_relays(8, 10)
    hop(2)
    take_near(c, 2, 2)
    hop(3)
    take_near(c, 4, 2)

    value = lost[0, r] + lost[1, r]
    part_hi = value.astype(BF16)
    left = value - part_hi.astype(F32)
    part_mid = left.astype(BF16)
    part_lo = (left - part_mid.astype(F32)).astype(BF16)
    scale = 1.0 / math.sqrt(order)
    w0, w1 = wavelet[0] * scale, wavelet[1] * scale
    for j in range(CHUNKS):
        s = big(j)
        spread = mm(hot_row[s], part_hi) + mm(hot_row[s], part_mid) + mm(hot_row[s], part_lo)
        q_copy(j).wait_recv()
        sc_copy(j).wait_recv()
        sib_copy(1, c1, j).wait_recv()
        total = part[c, s] + sib[1, s] + qrecv[s].astype(jnp.int32).astype(F32) * srecv[j, 0:1, :]
        dead = dead_ref[s] > 0.5
        real = jnp.where(dead, spread[:, :win], total[:, :win])
        imag = jnp.where(dead, spread[:, win:], total[:, win:])
        out[0, s] = wown[0, s].astype(F32) - (w0 * real - w1 * imag)
        out[1, s] = wown[1, s].astype(F32) - (w0 * imag + w1 * real)

    for which in range(3):
        for p in range(2):
            x_copy(which, p).wait_send()
    for j in range(CHUNKS):
        sib_copy(0, far0 + 1 - side, j).wait_send()
        sib_copy(1, c1, j).wait_send()
        q_copy(j).wait_send()
        sc_copy(j).wait_send()
    for b in range(grid):
        @pl.when((b > r) & (r < grid - 1))
        def _():
            up_copy(b).wait_send()

        @pl.when((b < r) & (r > 0))
        def _():
            down_copy(b).wait_send()

    @pl.when(jnp.logical_not(hub))
    def _():
        pat.wait_send()

    @pl.when(same)
    def _():
        @pl.loop(0, PIECES)
        def _(p):
            own_copy(p, 2).wait_send()
            own_copy(p, 1).wait_send()

            @pl.when(jnp.logical_not(hub))
            def _():
                own_copy(p, 0).wait_send()

        @pl.loop(0, LANE)
        def _(p):
            for i in range(2):
                cross_copy(far0 + i, p).wait_send()

                @pl.when(inner)
                def _():
                    pass_copy(far0 + i, p).wait_send()

    @pl.when(hub)
    def _():
        for i in range(2):
            for e in range(extra):
                for which in range(2):
                    hub_copy(i, e, which).wait_send()

    @pl.when(jnp.logical_not(same))
    def _():
        @pl.loop(0, PIECES)
        def _(p):
            own_copy(p, 0).wait_send()

        @pl.loop(0, LANE)
        def _(p):
            lane_copy(p, 2).wait_send()
            lane_copy(p, 1).wait_send()
            cross_copy(r1, p).wait_send()

        @pl.when(inner)
        def _():
            @pl.loop(0, PIECES)
            def _(p):
                for i in range(2):
                    fwd_copy(own0 + i, p).wait_send()
            for i in range(2):
                for e in range(extra):
                    fwd_copy(far0 + i, LANE + e).wait_send()


def make_fused(order):
    def local(traces, recv_live, missing, wavelet):
        tile = traces.shape[1]
        grid, dead_n = missing.shape
        win = 128
        recv = recv_live.reshape(grid, tile)
        dma, vmem = pltpu.SemaphoreType.DMA, pltpu.VMEM
        block = (2, tile, win)
        wide = (tile, 2 * win)
        scratch = [
            vmem((2, tile, tile), BF16),
            vmem(block, BF16), vmem(block, BF16), vmem(block, BF16),
            vmem((grid,) + block, BF16), vmem((2,) + block, BF16),
            vmem((2, dead_n, win), BF16), vmem((2, dead_n, win), BF16),
            vmem((grid,) + wide, F32), vmem((2,) + wide, F32),
            vmem(wide, jnp.int16), vmem(wide, jnp.int16),
            vmem((CHUNKS, 8, 2 * win), F32), vmem((CHUNKS, 8, 2 * win), F32),
            vmem((grid, 2, dead_n, tile), BF16),
            vmem((2, grid, dead_n, 2 * win), F32),
            vmem((grid, dead_n, 2 * win), F32), vmem((grid, dead_n, 2 * win), F32),
            vmem((tile, dead_n), BF16), vmem((tile, win), F32), vmem((tile, win), F32),
            dma((2,)), dma((1,)), dma((1,)), dma((3, 2)), dma((grid, 2)),
            dma((grid, PIECES)), dma((2, LANE)), dma((3, PIECES)), dma((2, PIECES - LANE, 2)),
            dma((grid, PIECES)), dma((2, LANE, 2)),
            dma((grid,)), dma((grid,)), dma((grid,)), dma((grid,)),
            dma((2, CHUNKS)), dma((2, CHUNKS)),
            dma((CHUNKS,)), dma((CHUNKS,)), dma((CHUNKS,)), dma((CHUNKS,)),
        ]
        whole = pl.BlockSpec(memory_space=pltpu.VMEM)
        return pl.pallas_call(
            functools.partial(fused_kernel, order),
            out_shape=jax.ShapeDtypeStruct(block, F32),
            in_specs=[
                pl.BlockSpec(memory_space=pl.ANY), whole, whole, whole,
                pl.BlockSpec(memory_space=pltpu.SMEM),
            ],
            out_specs=whole,
            scratch_shapes=scratch,
            compiler_params=pltpu.CompilerParams(
                collective_id=0, has_side_effects=True, vmem_limit_bytes=56 * 2**20
            ),
        )(traces, recv, missing, missing.T, wavelet)

    return local


def solution(mesh):
    in_specs = (P("freq", "row", "col"), P("freq"), P("freq", None), P("freq"))
    out_specs = P("freq", "row", "col")
    small = mesh.shape["row"] == 4 and mesh.shape["col"] == 4

    def run(traces, recv_live, missing, wavelet):
        local = (make_fused if small else make_local)(traces.shape[1])
        return jax.shard_map(
            local, mesh=mesh, in_specs=in_specs, out_specs=out_specs, check_vma=False
        )(traces, recv_live, missing, wavelet)

    return run
```

```python
import functools
import math

import jax
import jax.numpy as jnp
from jax import lax
from jax.experimental import pallas as pl
from jax.experimental.pallas import tpu as pltpu
from jax.sharding import PartitionSpec as P

F32 = jnp.float32
BF16 = jnp.bfloat16


def dot(first, second, dims=((1,), (0,)), **kw):
    return lax.dot_general(first, second, (dims, ((), ())), preferred_element_type=F32, **kw)


def make_local(order):
    def local(traces, recv_live, missing, wavelet):
        tile = traces.shape[1]
        grid = lax.axis_size("row")
        win = 128
        row = lax.axis_index("row")
        col = lax.axis_index("col")
        positions = jnp.arange(tile, dtype=jnp.int32)
        raw = traces[:, :, :win]
        gathered = lax.all_gather(raw, "row", axis=0, tiled=False)

        miss_row = lax.dynamic_index_in_dim(missing, row, 0, keepdims=False)
        miss_col = lax.dynamic_index_in_dim(missing, col, 0, keepdims=False)
        hot_row = positions[None, :] == miss_row[:, None]
        hot_col = positions[None, :] == miss_col[:, None]
        dead_row = jnp.any(hot_row, axis=0)
        dead_col = jnp.any(hot_col, axis=0)
        dead_win = jnp.any(missing[:, :, None] == positions[None, None, :win], axis=1)
        recv = (recv_live == 1).reshape(grid, tile)
        recv_row = lax.dynamic_index_in_dim(recv, row, 0, keepdims=False)
        recv_col = lax.dynamic_index_in_dim(recv, col, 0, keepdims=False)
        recv_miss_row = jnp.any(hot_row & recv_row[None, :], axis=1)
        recv_miss_col = jnp.any(hot_col & recv_col[None, :], axis=1)
        hot_row_b = hot_row.astype(BF16)
        hot_col_b = hot_col.astype(BF16)
        zero = jnp.zeros((), BF16)

        outgoing = jnp.stack([dot(hot_col_b, traces[p], ((1,), (1,))) for p in range(2)]).astype(BF16)
        route = [(r * grid + c, c * grid + r) for r in range(grid) for c in range(grid)]
        incoming = lax.ppermute(outgoing, ("row", "col"), route)
        dead_gather = lax.all_gather(outgoing[:, :, :win], "row", axis=0, tiled=False)

        swapped = lax.all_to_all(gathered, "col", split_axis=0, concat_axis=0, tiled=True)
        wide = jnp.transpose(swapped, (1, 2, 0, 3)).reshape(2, tile, grid * win)
        live_win = recv[:, :win].reshape(-1)
        keep = jnp.where(live_win[None, :] & ~dead_col[:, None], True, False)
        deads = jnp.transpose(dead_gather, (1, 2, 0, 3)).reshape(2, -1, grid * win)
        dead_keep = recv_miss_col[:, None] & ~dead_win.reshape(-1)[None, :]
        deads = jnp.where(dead_keep[None], deads, zero)
        window = [
            jnp.where(keep, wide[p], dot(hot_col_b, deads[p], ((0,), (0,))).astype(BF16))
            for p in range(2)
        ]
        masked = [jnp.where(recv_col[:, None], w, zero) for w in window]
        patched = jnp.where(recv_miss_row[None, :, None] & ~dead_col[None, None, :], incoming, zero)

        def product(left, right):
            first = jnp.concatenate([right[0], right[1]], axis=1)
            second = jnp.concatenate([-right[1], right[0]], axis=1)
            return dot(left[0], first) + dot(left[1], second)

        live = product(traces, masked)
        lost = product(patched, window)
        lost = dot(hot_row.astype(F32), lost, ((0,), (0,)), precision=lax.Precision.HIGHEST)
        partial = jnp.where(dead_row[:, None], lost, live)
        partial = jnp.transpose(partial.reshape(tile, 2, grid, win), (2, 1, 0, 3))
        total = lax.psum_scatter(partial, "col", scatter_dimension=0, tiled=True)[0]
        scale = 1.0 / math.sqrt(order)
        real = (wavelet[0] * total[0] - wavelet[1] * total[1]) * scale
        imag = (wavelet[0] * total[1] + wavelet[1] * total[0]) * scale
        own_in = lax.dynamic_index_in_dim(recv[:, :win], col, 0, keepdims=False)
        own_dead = jnp.where(
            recv_miss_row[None, :, None] & ~dead_col[None, None, :win], incoming[:, :, :win], zero
        )
        own = [
            jnp.where(
                dead_row[:, None],
                dot(hot_row_b, own_dead[p], ((0,), (0,))),
                jnp.where(own_in[None, :], raw[p], zero).astype(F32),
            )
            for p in range(2)
        ]
        return jnp.stack([own[0] - real, own[1] - imag])

    return local


MESH = pl.DeviceIdType.MESH
PIECES = 6
LANE = 4
CHUNKS = 3


def nt(first, second):
    return lax.dot_general(first, second, (((1,), (1,)), ((), ())), preferred_element_type=F32)


def mm(first, second):
    return jnp.dot(first, second, preferred_element_type=F32)


def fused_kernel(
    order, traces, recv, miss, wavelet, out,
    tile_ref, ws, wown, wlive, wbuf, tbuf, psend, precv, part, sib, qsend, qrecv, ssend, srecv,
    xt, lost, up_in, down_in, hot_col, hot_row, dead_ref, recv_rows,
    tile_sem, pat_s, pat_r, x_s, x_r, w_r, t_r, own_s, hub_s, fwd_s, tran_s,
    up_s, up_r, down_s, down_r, sib_s, sib_r, q_s, q_r, sc_s, sc_r,
):
    f = lax.axis_index("freq")
    r = lax.axis_index("row")
    c = lax.axis_index("col")
    grid = 4
    tile, win = tile_ref.shape[1], wown.shape[2]
    dead_n = xt.shape[2]
    rows = tile // PIECES
    extra = PIECES - LANE
    chunk = tile // CHUNKS
    rh, ch = r // 2, c // 2
    same = rh == ch
    hub = r == c
    inner = (r == 1) | (r == 2)
    r1 = r + 1 - 2 * (r % 2)
    c1 = c + 1 - 2 * (c % 2)
    cx = (c + 2) % 4
    mid_of_r = 2 - rh
    near_edge = 3 * rh
    far0 = 2 * (1 - ch)
    own0 = 2 * ch

    def sub(p):
        return pl.ds(pl.multiple_of(p * rows, rows), rows)

    def big(j):
        return pl.ds(pl.multiple_of(j * chunk, chunk), chunk)

    def rc(src, dst, ssem, rsem, dev):
        return pltpu.make_async_remote_copy(
            src_ref=src, dst_ref=dst, send_sem=ssem, recv_sem=rsem,
            device_id=(f, dev[0], dev[1]), device_id_type=MESH,
        )

    def own_copy(p, which):
        dev = [(r, r), (r1, r), (mid_of_r, r)][which]
        return rc(ws.at[:, sub(p)], wbuf.at[c, :, sub(p)], own_s.at[which, p], w_r.at[c, p], dev)

    def lane_copy(p, which):
        dev = [None, (r1, c), (mid_of_r, c)][which]
        slot = r % 2
        return rc(ws.at[:, sub(p)], tbuf.at[slot, :, sub(p)], own_s.at[which, p], t_r.at[slot, p], dev)

    def hub_copy(i, e, which):
        b, p = far0 + i, LANE + e
        dev = [(r1, r), (mid_of_r, r)][which]
        return rc(wbuf.at[b, :, sub(p)], wbuf.at[b, :, sub(p)], hub_s.at[i, e, which], w_r.at[b, p], dev)

    def fwd_copy(b, p):
        return rc(wbuf.at[b, :, sub(p)], wbuf.at[b, :, sub(p)], fwd_s.at[b, p], w_r.at[b, p], (near_edge, c))

    def cross_copy(k, p):
        slot = k % 2
        return rc(tbuf.at[slot, :, sub(p)], wbuf.at[c, :, sub(p)], tran_s.at[slot, p, 0], w_r.at[c, p], (r, k))

    def pass_copy(k, p):
        slot = k % 2
        return rc(tbuf.at[slot, :, sub(p)], tbuf.at[slot, :, sub(p)], tran_s.at[slot, p, 1], t_r.at[slot, p], (near_edge, c))

    def wait_w(b, p):
        rc(wbuf.at[b, :, sub(p)], wbuf.at[b, :, sub(p)], fwd_s.at[b, p], w_r.at[b, p], (r, c1)).wait_recv()

    def wait_t(slot, p):
        rc(tbuf.at[slot, :, sub(p)], tbuf.at[slot, :, sub(p)], tran_s.at[slot, p, 0], t_r.at[slot, p], (r, c1)).wait_recv()

    def x_copy(which, p):
        src = [c, c, cx][which]
        dev = [(r, c1), (r, cx), (r, c1)][which]
        return rc(xt.at[src, p], xt.at[src, p], x_s.at[which, p], x_r.at[src, p], dev)

    def wait_x(b, p):
        rc(xt.at[b, p], xt.at[b, p], x_s.at[0, p], x_r.at[b, p], (r, c1)).wait_recv()

    def up_copy(b):
        return rc(lost.at[0, b], up_in.at[b], up_s.at[b], up_r.at[b], (jnp.minimum(r + 1, grid - 1), c))

    def down_copy(b):
        return rc(lost.at[1, b], down_in.at[b], down_s.at[b], down_r.at[b], (jnp.maximum(r - 1, 0), c))

    def sib_copy(phase, b, j):
        return rc(part.at[b, big(j)], sib.at[phase, big(j)], sib_s.at[phase, j], sib_r.at[phase, j], (r, c1))

    def q_copy(j):
        return rc(qsend.at[big(j)], qrecv.at[big(j)], q_s.at[j], q_r.at[j], (r, cx))

    def sc_copy(j):
        return rc(ssend.at[j], srecv.at[j], sc_s.at[j], sc_r.at[j], (r, cx))

    pat = rc(psend, precv, pat_s.at[0], pat_r.at[0], (c, r))

    head = pltpu.make_async_copy(traces.at[:, pl.ds(0, win)], tile_ref.at[:, pl.ds(0, win)], tile_sem.at[0])
    rest = pltpu.make_async_copy(
        traces.at[:, pl.ds(win, tile - win)], tile_ref.at[:, pl.ds(win, tile - win)], tile_sem.at[1])
    head.start()
    rest.start()
    barrier = pltpu.get_barrier_semaphore()
    for n in range(1, grid * grid):
        other = (r * grid + c + n) % (grid * grid)
        pl.semaphore_signal(
            barrier, inc=1, device_id=(f, other // grid, other % grid), device_id_type=MESH)

    span = tile // win

    def lanes_of(block):
        return [recv[pl.ds(block * span + j, 1), :] for j in range(span)]

    def column(row):
        shape = (dead_n, dead_n)
        diagonal = lax.broadcasted_iota(jnp.int32, shape, 0) == lax.broadcasted_iota(jnp.int32, shape, 1)
        return jnp.sum(jnp.where(diagonal, jnp.broadcast_to(row, shape), 0), axis=1, keepdims=True)

    miss_row = miss[pl.ds(r, 1), :]
    recv_c = lanes_of(c)
    miss_c = column(miss[pl.ds(c, 1), :])
    place = lax.broadcasted_iota(jnp.int32, (dead_n, win), 1)
    for j in range(span):
        hot_col[:, j * win:(j + 1) * win] = jnp.where(
            (place + j * win == miss_c) & (recv_c[j] == 1), 1.0, 0.0).astype(BF16)
    head_hot = jnp.where(place == column(miss_row), 1.0, 0.0)
    live_q = 1.0 - jnp.max(head_hot, axis=0, keepdims=True)
    recv_q = jnp.where(recv_c[0] == 1, 1.0, 0.0)

    head.wait()
    for p in range(2):
        psend[p] = (nt(hot_col[...], tile_ref[p, :win, :]) * live_q).astype(BF16)
    pl.semaphore_wait(barrier, grid * grid - 1)

    @pl.when(hub)
    def _():
        precv[...] = psend[...]

    @pl.when(jnp.logical_not(hub))
    def _():
        pat.start()

    recv_r = lanes_of(r)
    for j in range(span):
        lane = jnp.where(recv_r[j] == 1, 1.0, 0.0)
        recv_rows[pl.ds(j * win, win), :] = jnp.transpose(jnp.broadcast_to(lane, (win, win)))
    ones = jnp.ones((dead_n, win), BF16)
    for j in range(CHUNKS):
        spot = lax.broadcasted_iota(jnp.int32, (chunk, dead_n), 0) + j * chunk
        hot = jnp.where(spot == miss_row, 1.0, 0.0).astype(BF16)
        hot_row[pl.ds(j * chunk, chunk), :] = hot
        dead_ref[pl.ds(j * chunk, chunk), :] = mm(hot, ones)
    rest.wait()
    for p in range(2):
        for j in range(CHUNKS):
            s = pl.ds(j * chunk, chunk)
            raw = tile_ref[p, s, :win].astype(F32) * recv_q
            wlive[p, s] = jnp.where(dead_ref[s] > 0.5, 0.0, raw).astype(BF16)

    @pl.when(jnp.logical_not(hub))
    def _():
        pat.wait_recv()

    for p in range(2):
        for j in range(CHUNKS):
            s = pl.ds(j * chunk, chunk)
            full = wlive[p, s].astype(F32) + mm(hot_row[s], precv[p])
            wown[p, s] = full.astype(BF16)
            ws[p, s] = (full * recv_rows[s]).astype(BF16)

    @pl.when(hub)
    def _():
        wbuf[c] = ws[...]

    @pl.when(same & jnp.logical_not(hub))
    def _():
        @pl.loop(0, PIECES)
        def _(p):
            own_copy(p, 2).start()
            own_copy(p, 1).start()
            own_copy(p, 0).start()

    @pl.when(jnp.logical_not(same))
    def _():
        @pl.loop(LANE, PIECES)
        def _(p):
            own_copy(p, 0).start()

        @pl.loop(0, LANE)
        def _(p):
            lane_copy(p, 2).start()
            lane_copy(p, 1).start()
            own_copy(p, 0).start()


    for p in range(2):
        for j in range(CHUNKS):
            s = pl.ds(j * chunk, chunk)
            xt[c, p, :, s] = nt(hot_col[...], tile_ref[p, s, :]).astype(BF16)
        x_copy(1, p).start()
        x_copy(0, p).start()

    @pl.when(hub)
    def _():
        own_copy(0, 2).start()
        own_copy(0, 1).start()
        for e in range(extra):
            for i in range(2):
                wait_w(far0 + i, LANE + e)
                for which in range(2):
                    hub_copy(i, e, which).start()

        @pl.loop(1, PIECES)
        def _(p):
            own_copy(p, 2).start()
            own_copy(p, 1).start()

    relay = inner & jnp.logical_not(same)

    def accumulate(b, p, count, fresh=False):
        k = pl.ds(pl.multiple_of(p * rows, rows), count * rows)
        re, im = wbuf[b, 0, k, :], wbuf[b, 1, k, :]
        first = jnp.concatenate([re, im], axis=1)
        second = jnp.concatenate([-im, re], axis=1)

        @pl.loop(0, CHUNKS)
        def _(j):
            s = big(j)
            value = mm(tile_ref[0, s, k], first) + mm(tile_ref[1, s, k], second)
            part[b, s] = value if fresh else part[b, s] + value

    def relay_piece(b, p):
        @pl.when(relay)
        def _():
            wait_w(b, p)
            fwd_copy(b, p).start()

    def transit(p):
        @pl.when(same)
        def _():
            for i in range(2):
                k = far0 + i
                wait_t(i, p)

                @pl.when(inner)
                def _():
                    pass_copy(k, p).start()
                cross_copy(k, p).start()

        @pl.when(jnp.logical_not(same))
        def _():
            wait_t(r1 % 2, p)
            cross_copy(r1, p).start()

    def take_far(b, p, count, fresh=False):
        for n in range(count):
            if p + n < LANE:
                wait_w(b, p + n)
            else:
                @pl.when(jnp.logical_not(hub | relay))
                def _():
                    wait_w(b, p + n)
        accumulate(b, p, count, fresh)

    def take_near(b, p, count, fresh=False):
        for n in range(count):
            @pl.when(jnp.logical_not(relay | (hub & (b == c))))
            def _():
                wait_w(b, p + n)
        accumulate(b, p, count, fresh)

    def hop(step):
        @pl.when(r == step)
        def _():
            for b in range(step, grid):
                up_copy(b).wait_recv()
            for b in range(step, grid):
                lost[0, b] = lost[0, b] + up_in[b]
            for b in range(step + 1, grid):
                up_copy(b).start()

        @pl.when(r == grid - 1 - step)
        def _():
            for b in range(0, grid - step):
                down_copy(b).wait_recv()
            for b in range(0, grid - step):
                lost[1, b] = lost[1, b] + down_in[b]
            for b in range(0, grid - 1 - step):
                down_copy(b).start()

    side = c % 2
    far_own, far_sib = far0 + side, far0 + 1 - side
    hub_order = [(c, 0)] + [(far0 + i, LANE + e) for e in range(extra) for i in range(2)] + [(c, p) for p in range(1, PIECES)]

    def near_relays(first, last):
        for t in range(first, last):
            if t < PIECES:
                relay_piece(c1, t)
            relay_piece(*hub_order[t])

    transit(0)
    near_relays(0, 1)
    transit(1)
    near_relays(1, 2)
    transit(2)
    near_relays(2, 3)
    take_far(far_sib, 0, 2, True)
    take_far(far_own, 0, 2, True)
    transit(3)
    near_relays(3, 4)

    for p in range(2):
        wait_x(cx, p)
        x_copy(2, p).start()
    take_far(far_sib, 2, 2)
    take_far(far_own, 2, 2)
    near_relays(4, 5)
    re, im = wlive[0], wlive[1]
    first = jnp.concatenate([re, im], axis=1)
    second = jnp.concatenate([-im, re], axis=1)
    for p in range(2):
        wait_x(c1, p)
        wait_x((c1 + 2) % 4, p)
    for b in range(grid):
        value = mm(xt[b, 0], first) + mm(xt[b, 1], second)
        lost[0, b] = value
        lost[1, b] = value * jnp.where(r == b, 0.0, 1.0)
    for b in range(1, grid):
        @pl.when((r == 0))
        def _():
            up_copy(b).start()

        @pl.when((r == grid - 1))
        def _():
            down_copy(grid - 1 - b).start()

    take_far(far_sib, LANE, extra)
    for j in range(CHUNKS):
        sib_copy(0, far_sib, j).start()
    take_far(far_own, LANE, extra)
    for j in range(CHUNKS):
        s = big(j)
        sib_copy(0, far_sib, j).wait_recv()
        value = part[far_own, s] + sib[0, s]
        top = jnp.max(jnp.abs(value), axis=0, keepdims=True)
        ratio = jnp.where(top > 0.0, 32767.0 / jnp.maximum(top, 1e-30), 0.0)
        qsend[s] = jnp.round(value * ratio).astype(jnp.int32).astype(jnp.int16)
        ssend[j] = jnp.broadcast_to(top * (1.0 / 32767.0), ssend.shape[1:])
        q_copy(j).start()
        sc_copy(j).start()
    near_relays(5, 6)
    take_near(c1, 0, 3, True)
    near_relays(6, 7)
    hop(1)
    take_near(c1, 3, 3)
    for j in range(CHUNKS):
        sib_copy(1, c1, j).start()
    near_relays(7, 8)
    take_near(c, 0, 2, True)
    near_relays(8, 10)
    hop(2)
    take_near(c, 2, 2)
    hop(3)
    take_near(c, 4, 2)

    value = lost[0, r] + lost[1, r]
    part_hi = value.astype(BF16)
    left = value - part_hi.astype(F32)
    part_mid = left.astype(BF16)
    part_lo = (left - part_mid.astype(F32)).astype(BF16)
    scale = 1.0 / math.sqrt(order)
    w0, w1 = wavelet[0] * scale, wavelet[1] * scale
    for j in range(CHUNKS):
        s = big(j)
        spread = mm(hot_row[s], part_hi) + mm(hot_row[s], part_mid) + mm(hot_row[s], part_lo)
        q_copy(j).wait_recv()
        sc_copy(j).wait_recv()
        sib_copy(1, c1, j).wait_recv()
        total = part[c, s] + sib[1, s] + qrecv[s].astype(jnp.int32).astype(F32) * srecv[j, 0:1, :]
        dead = dead_ref[s] > 0.5
        real = jnp.where(dead, spread[:, :win], total[:, :win])
        imag = jnp.where(dead, spread[:, win:], total[:, win:])
        out[0, s] = wown[0, s].astype(F32) - (w0 * real - w1 * imag)
        out[1, s] = wown[1, s].astype(F32) - (w0 * imag + w1 * real)

    for which in range(3):
        for p in range(2):
            x_copy(which, p).wait_send()
    for j in range(CHUNKS):
        sib_copy(0, far0 + 1 - side, j).wait_send()
        sib_copy(1, c1, j).wait_send()
        q_copy(j).wait_send()
        sc_copy(j).wait_send()
    for b in range(grid):
        @pl.when((b > r) & (r < grid - 1))
        def _():
            up_copy(b).wait_send()

        @pl.when((b < r) & (r > 0))
        def _():
            down_copy(b).wait_send()

    @pl.when(jnp.logical_not(hub))
    def _():
        pat.wait_send()

    @pl.when(same)
    def _():
        @pl.loop(0, PIECES)
        def _(p):
            own_copy(p, 2).wait_send()
            own_copy(p, 1).wait_send()

            @pl.when(jnp.logical_not(hub))
            def _():
                own_copy(p, 0).wait_send()

        @pl.loop(0, LANE)
        def _(p):
            for i in range(2):
                cross_copy(far0 + i, p).wait_send()

                @pl.when(inner)
                def _():
                    pass_copy(far0 + i, p).wait_send()

    @pl.when(hub)
    def _():
        for i in range(2):
            for e in range(extra):
                for which in range(2):
                    hub_copy(i, e, which).wait_send()

    @pl.when(jnp.logical_not(same))
    def _():
        @pl.loop(0, PIECES)
        def _(p):
            own_copy(p, 0).wait_send()

        @pl.loop(0, LANE)
        def _(p):
            lane_copy(p, 2).wait_send()
            lane_copy(p, 1).wait_send()
            cross_copy(r1, p).wait_send()

        @pl.when(inner)
        def _():
            @pl.loop(0, PIECES)
            def _(p):
                for i in range(2):
                    fwd_copy(own0 + i, p).wait_send()
            for i in range(2):
                for e in range(extra):
                    fwd_copy(far0 + i, LANE + e).wait_send()


def make_fused(order):
    def local(traces, recv_live, missing, wavelet):
        tile = traces.shape[1]
        grid, dead_n = missing.shape
        win = 128
        recv = recv_live.reshape(-1, win)
        dma, vmem = pltpu.SemaphoreType.DMA, pltpu.VMEM
        block = (2, tile, win)
        wide = (tile, 2 * win)
        scratch = [
            vmem((2, tile, tile), BF16),
            vmem(block, BF16), vmem(block, BF16), vmem(block, BF16),
            vmem((grid,) + block, BF16), vmem((2,) + block, BF16),
            vmem((2, dead_n, win), BF16), vmem((2, dead_n, win), BF16),
            vmem((grid,) + wide, F32), vmem((2,) + wide, F32),
            vmem(wide, jnp.int16), vmem(wide, jnp.int16),
            vmem((CHUNKS, 8, 2 * win), F32), vmem((CHUNKS, 8, 2 * win), F32),
            vmem((grid, 2, dead_n, tile), BF16),
            vmem((2, grid, dead_n, 2 * win), F32),
            vmem((grid, dead_n, 2 * win), F32), vmem((grid, dead_n, 2 * win), F32),
            vmem((dead_n, tile), BF16), vmem((tile, dead_n), BF16), vmem((tile, win), F32), vmem((tile, win), F32),
            dma((2,)), dma((1,)), dma((1,)), dma((3, 2)), dma((grid, 2)),
            dma((grid, PIECES)), dma((2, LANE)), dma((3, PIECES)), dma((2, PIECES - LANE, 2)),
            dma((grid, PIECES)), dma((2, LANE, 2)),
            dma((grid,)), dma((grid,)), dma((grid,)), dma((grid,)),
            dma((2, CHUNKS)), dma((2, CHUNKS)),
            dma((CHUNKS,)), dma((CHUNKS,)), dma((CHUNKS,)), dma((CHUNKS,)),
        ]
        whole = pl.BlockSpec(memory_space=pltpu.VMEM)
        return pl.pallas_call(
            functools.partial(fused_kernel, order),
            out_shape=jax.ShapeDtypeStruct(block, F32),
            in_specs=[
                pl.BlockSpec(memory_space=pl.ANY), whole, whole,
                pl.BlockSpec(memory_space=pltpu.SMEM),
            ],
            out_specs=whole,
            scratch_shapes=scratch,
            compiler_params=pltpu.CompilerParams(
                collective_id=0, has_side_effects=True, vmem_limit_bytes=56 * 2**20
            ),
        )(traces, recv, missing, wavelet)

    return local


def solution(mesh):
    in_specs = (P("freq", "row", "col"), P("freq"), P("freq", None), P("freq"))
    out_specs = P("freq", "row", "col")
    small = mesh.shape["row"] == 4 and mesh.shape["col"] == 4

    def run(traces, recv_live, missing, wavelet):
        local = (make_fused if small else make_local)(traces.shape[1])
        return jax.shard_map(
            local, mesh=mesh, in_specs=in_specs, out_specs=out_specs, check_vma=False
        )(traces, recv_live, missing, wavelet)

    return run
```

```python
import functools
import math

import jax
import jax.numpy as jnp
from jax import lax
from jax.experimental import pallas as pl
from jax.experimental.pallas import tpu as pltpu
from jax.sharding import PartitionSpec as P

F32 = jnp.float32
BF16 = jnp.bfloat16


def dot(first, second, dims=((1,), (0,)), **kw):
    return lax.dot_general(first, second, (dims, ((), ())), preferred_element_type=F32, **kw)


def make_local(order):
    def local(traces, recv_live, missing, wavelet):
        tile = traces.shape[1]
        grid = lax.axis_size("row")
        win = 128
        row = lax.axis_index("row")
        col = lax.axis_index("col")
        positions = jnp.arange(tile, dtype=jnp.int32)
        raw = traces[:, :, :win]
        gathered = lax.all_gather(raw, "row", axis=0, tiled=False)

        miss_row = lax.dynamic_index_in_dim(missing, row, 0, keepdims=False)
        miss_col = lax.dynamic_index_in_dim(missing, col, 0, keepdims=False)
        hot_row = positions[None, :] == miss_row[:, None]
        hot_col = positions[None, :] == miss_col[:, None]
        dead_row = jnp.any(hot_row, axis=0)
        dead_col = jnp.any(hot_col, axis=0)
        dead_win = jnp.any(missing[:, :, None] == positions[None, None, :win], axis=1)
        recv = (recv_live == 1).reshape(grid, tile)
        recv_row = lax.dynamic_index_in_dim(recv, row, 0, keepdims=False)
        recv_col = lax.dynamic_index_in_dim(recv, col, 0, keepdims=False)
        recv_miss_row = jnp.any(hot_row & recv_row[None, :], axis=1)
        recv_miss_col = jnp.any(hot_col & recv_col[None, :], axis=1)
        hot_row_b = hot_row.astype(BF16)
        hot_col_b = hot_col.astype(BF16)
        zero = jnp.zeros((), BF16)

        outgoing = jnp.stack([dot(hot_col_b, traces[p], ((1,), (1,))) for p in range(2)]).astype(BF16)
        route = [(r * grid + c, c * grid + r) for r in range(grid) for c in range(grid)]
        incoming = lax.ppermute(outgoing, ("row", "col"), route)
        dead_gather = lax.all_gather(outgoing[:, :, :win], "row", axis=0, tiled=False)

        swapped = lax.all_to_all(gathered, "col", split_axis=0, concat_axis=0, tiled=True)
        wide = jnp.transpose(swapped, (1, 2, 0, 3)).reshape(2, tile, grid * win)
        live_win = recv[:, :win].reshape(-1)
        keep = jnp.where(live_win[None, :] & ~dead_col[:, None], True, False)
        deads = jnp.transpose(dead_gather, (1, 2, 0, 3)).reshape(2, -1, grid * win)
        dead_keep = recv_miss_col[:, None] & ~dead_win.reshape(-1)[None, :]
        deads = jnp.where(dead_keep[None], deads, zero)
        window = [
            jnp.where(keep, wide[p], dot(hot_col_b, deads[p], ((0,), (0,))).astype(BF16))
            for p in range(2)
        ]
        masked = [jnp.where(recv_col[:, None], w, zero) for w in window]
        patched = jnp.where(recv_miss_row[None, :, None] & ~dead_col[None, None, :], incoming, zero)

        def product(left, right):
            first = jnp.concatenate([right[0], right[1]], axis=1)
            second = jnp.concatenate([-right[1], right[0]], axis=1)
            return dot(left[0], first) + dot(left[1], second)

        live = product(traces, masked)
        lost = product(patched, window)
        lost = dot(hot_row.astype(F32), lost, ((0,), (0,)), precision=lax.Precision.HIGHEST)
        partial = jnp.where(dead_row[:, None], lost, live)
        partial = jnp.transpose(partial.reshape(tile, 2, grid, win), (2, 1, 0, 3))
        total = lax.psum_scatter(partial, "col", scatter_dimension=0, tiled=True)[0]
        scale = 1.0 / math.sqrt(order)
        real = (wavelet[0] * total[0] - wavelet[1] * total[1]) * scale
        imag = (wavelet[0] * total[1] + wavelet[1] * total[0]) * scale
        own_in = lax.dynamic_index_in_dim(recv[:, :win], col, 0, keepdims=False)
        own_dead = jnp.where(
            recv_miss_row[None, :, None] & ~dead_col[None, None, :win], incoming[:, :, :win], zero
        )
        own = [
            jnp.where(
                dead_row[:, None],
                dot(hot_row_b, own_dead[p], ((0,), (0,))),
                jnp.where(own_in[None, :], raw[p], zero).astype(F32),
            )
            for p in range(2)
        ]
        return jnp.stack([own[0] - real, own[1] - imag])

    return local


MESH = pl.DeviceIdType.MESH
PIECES = 4
LANE = 3
CHUNKS = 3


def nt(first, second):
    return lax.dot_general(first, second, (((1,), (1,)), ((), ())), preferred_element_type=F32)


def mm(first, second):
    return jnp.dot(first, second, preferred_element_type=F32)


def fused_kernel(
    order, traces, recv, miss, wavelet, out,
    tile_ref, ws, wown, wlive, wbuf, tbuf, psend, precv, part, sib, qsend, qrecv, ssend, srecv,
    xt, lost, up_in, down_in, hot_col, hot_row, dead_ref, recv_rows,
    tile_sem, pat_s, pat_r, x_s, x_r, w_r, t_r, own_s, hub_s, fwd_s, tran_s,
    up_s, up_r, down_s, down_r, sib_s, sib_r, q_s, q_r, sc_s, sc_r,
):
    f = lax.axis_index("freq")
    r = lax.axis_index("row")
    c = lax.axis_index("col")
    grid = 4
    tile, win = tile_ref.shape[1], wown.shape[2]
    dead_n = xt.shape[2]
    rows = tile // PIECES
    extra = PIECES - LANE
    chunk = tile // CHUNKS
    rh, ch = r // 2, c // 2
    same = rh == ch
    hub = r == c
    inner = (r == 1) | (r == 2)
    r1 = r + 1 - 2 * (r % 2)
    c1 = c + 1 - 2 * (c % 2)
    cx = (c + 2) % 4
    mid_of_r = 2 - rh
    near_edge = 3 * rh
    far0 = 2 * (1 - ch)
    own0 = 2 * ch

    def sub(p):
        return pl.ds(pl.multiple_of(p * rows, rows), rows)

    def big(j):
        return pl.ds(pl.multiple_of(j * chunk, chunk), chunk)

    def rc(src, dst, ssem, rsem, dev):
        return pltpu.make_async_remote_copy(
            src_ref=src, dst_ref=dst, send_sem=ssem, recv_sem=rsem,
            device_id=(f, dev[0], dev[1]), device_id_type=MESH,
        )

    def own_copy(p, which):
        dev = [(r, r), (r1, r), (mid_of_r, r)][which]
        return rc(ws.at[:, sub(p)], wbuf.at[c, :, sub(p)], own_s.at[which, p], w_r.at[c, p], dev)

    def lane_copy(p, which):
        dev = [None, (r1, c), (mid_of_r, c)][which]
        slot = r % 2
        return rc(ws.at[:, sub(p)], tbuf.at[slot, :, sub(p)], own_s.at[which, p], t_r.at[slot, p], dev)

    def hub_copy(i, e, which):
        b, p = far0 + i, LANE + e
        dev = [(r1, r), (mid_of_r, r)][which]
        return rc(wbuf.at[b, :, sub(p)], wbuf.at[b, :, sub(p)], hub_s.at[i, e, which], w_r.at[b, p], dev)

    def fwd_copy(b, p):
        return rc(wbuf.at[b, :, sub(p)], wbuf.at[b, :, sub(p)], fwd_s.at[b, p], w_r.at[b, p], (near_edge, c))

    def cross_copy(k, p):
        slot = k % 2
        return rc(tbuf.at[slot, :, sub(p)], wbuf.at[c, :, sub(p)], tran_s.at[slot, p, 0], w_r.at[c, p], (r, k))

    def pass_copy(k, p):
        slot = k % 2
        return rc(tbuf.at[slot, :, sub(p)], tbuf.at[slot, :, sub(p)], tran_s.at[slot, p, 1], t_r.at[slot, p], (near_edge, c))

    def wait_w(b, p):
        rc(wbuf.at[b, :, sub(p)], wbuf.at[b, :, sub(p)], fwd_s.at[b, p], w_r.at[b, p], (r, c1)).wait_recv()

    def wait_t(slot, p):
        rc(tbuf.at[slot, :, sub(p)], tbuf.at[slot, :, sub(p)], tran_s.at[slot, p, 0], t_r.at[slot, p], (r, c1)).wait_recv()

    def x_copy(which, p):
        src = [c, c, cx][which]
        dev = [(r, c1), (r, cx), (r, c1)][which]
        return rc(xt.at[src, p], xt.at[src, p], x_s.at[which, p], x_r.at[src, p], dev)

    def wait_x(b, p):
        rc(xt.at[b, p], xt.at[b, p], x_s.at[0, p], x_r.at[b, p], (r, c1)).wait_recv()

    def up_copy(b):
        return rc(lost.at[0, b], up_in.at[b], up_s.at[b], up_r.at[b], (jnp.minimum(r + 1, grid - 1), c))

    def down_copy(b):
        return rc(lost.at[1, b], down_in.at[b], down_s.at[b], down_r.at[b], (jnp.maximum(r - 1, 0), c))

    def sib_copy(phase, b, j):
        return rc(part.at[b, big(j)], sib.at[phase, big(j)], sib_s.at[phase, j], sib_r.at[phase, j], (r, c1))

    def q_copy(j):
        return rc(qsend.at[big(j)], qrecv.at[big(j)], q_s.at[j], q_r.at[j], (r, cx))

    def sc_copy(j):
        return rc(ssend.at[j], srecv.at[j], sc_s.at[j], sc_r.at[j], (r, cx))

    pat = rc(psend, precv, pat_s.at[0], pat_r.at[0], (c, r))

    head = pltpu.make_async_copy(traces.at[:, pl.ds(0, win)], tile_ref.at[:, pl.ds(0, win)], tile_sem.at[0])
    rest = pltpu.make_async_copy(
        traces.at[:, pl.ds(win, tile - win)], tile_ref.at[:, pl.ds(win, tile - win)], tile_sem.at[1])
    head.start()
    rest.start()
    barrier = pltpu.get_barrier_semaphore()
    for n in range(1, grid * grid):
        other = (r * grid + c + n) % (grid * grid)
        pl.semaphore_signal(
            barrier, inc=1, device_id=(f, other // grid, other % grid), device_id_type=MESH)

    span = tile // win

    def lanes_of(block):
        return [recv[pl.ds(block * span + j, 1), :] for j in range(span)]

    def column(row):
        shape = (dead_n, dead_n)
        diagonal = lax.broadcasted_iota(jnp.int32, shape, 0) == lax.broadcasted_iota(jnp.int32, shape, 1)
        return jnp.sum(jnp.where(diagonal, jnp.broadcast_to(row, shape), 0), axis=1, keepdims=True)

    miss_row = miss[pl.ds(r, 1), :]
    recv_c = lanes_of(c)
    miss_c = column(miss[pl.ds(c, 1), :])
    place = lax.broadcasted_iota(jnp.int32, (dead_n, win), 1)
    for j in range(span):
        hot_col[:, j * win:(j + 1) * win] = jnp.where(
            (place + j * win == miss_c) & (recv_c[j] == 1), 1.0, 0.0).astype(BF16)
    head_hot = jnp.where(place == column(miss_row), 1.0, 0.0)
    live_q = 1.0 - jnp.max(head_hot, axis=0, keepdims=True)
    recv_q = jnp.where(recv_c[0] == 1, 1.0, 0.0)

    head.wait()
    for p in range(2):
        psend[p] = (nt(hot_col[...], tile_ref[p, :win, :]) * live_q).astype(BF16)
    pl.semaphore_wait(barrier, grid * grid - 1)

    @pl.when(hub)
    def _():
        precv[...] = psend[...]

    @pl.when(jnp.logical_not(hub))
    def _():
        pat.start()

    recv_r = lanes_of(r)
    for j in range(span):
        lane = jnp.where(recv_r[j] == 1, 1.0, 0.0)
        recv_rows[pl.ds(j * win, win), :] = jnp.transpose(jnp.broadcast_to(lane, (win, win)))
    ones = jnp.ones((dead_n, win), BF16)
    for j in range(CHUNKS):
        spot = lax.broadcasted_iota(jnp.int32, (chunk, dead_n), 0) + j * chunk
        hot = jnp.where(spot == miss_row, 1.0, 0.0).astype(BF16)
        hot_row[pl.ds(j * chunk, chunk), :] = hot
        dead_ref[pl.ds(j * chunk, chunk), :] = mm(hot, ones)
    rest.wait()
    for p in range(2):
        for j in range(CHUNKS):
            s = pl.ds(j * chunk, chunk)
            raw = tile_ref[p, s, :win].astype(F32) * recv_q
            wlive[p, s] = jnp.where(dead_ref[s] > 0.5, 0.0, raw).astype(BF16)

    @pl.when(jnp.logical_not(hub))
    def _():
        pat.wait_recv()

    for p in range(2):
        for j in range(CHUNKS):
            s = pl.ds(j * chunk, chunk)
            full = wlive[p, s].astype(F32) + mm(hot_row[s], precv[p])
            wown[p, s] = full.astype(BF16)
            ws[p, s] = (full * recv_rows[s]).astype(BF16)

    @pl.when(hub)
    def _():
        wbuf[c] = ws[...]

    @pl.when(same & jnp.logical_not(hub))
    def _():
        @pl.loop(0, PIECES)
        def _(p):
            own_copy(p, 2).start()
            own_copy(p, 1).start()
            own_copy(p, 0).start()

    @pl.when(jnp.logical_not(same))
    def _():
        @pl.loop(LANE, PIECES)
        def _(p):
            own_copy(p, 0).start()

        @pl.loop(0, LANE)
        def _(p):
            lane_copy(p, 2).start()
            lane_copy(p, 1).start()
            own_copy(p, 0).start()


    for p in range(2):
        for j in range(CHUNKS):
            s = pl.ds(j * chunk, chunk)
            xt[c, p, :, s] = nt(hot_col[...], tile_ref[p, s, :]).astype(BF16)
        x_copy(1, p).start()
        x_copy(0, p).start()

    @pl.when(hub)
    def _():
        own_copy(0, 2).start()
        own_copy(0, 1).start()
        for e in range(extra):
            for i in range(2):
                wait_w(far0 + i, LANE + e)
                for which in range(2):
                    hub_copy(i, e, which).start()

        @pl.loop(1, PIECES)
        def _(p):
            own_copy(p, 2).start()
            own_copy(p, 1).start()

    relay = inner & jnp.logical_not(same)

    def accumulate(b, p, count, fresh=False):
        k = pl.ds(pl.multiple_of(p * rows, rows), count * rows)
        re, im = wbuf[b, 0, k, :], wbuf[b, 1, k, :]
        first = jnp.concatenate([re, im], axis=1)
        second = jnp.concatenate([-im, re], axis=1)

        @pl.loop(0, CHUNKS)
        def _(j):
            s = big(j)
            value = mm(tile_ref[0, s, k], first) + mm(tile_ref[1, s, k], second)
            part[b, s] = value if fresh else part[b, s] + value

    def relay_piece(b, p):
        @pl.when(relay)
        def _():
            wait_w(b, p)
            fwd_copy(b, p).start()

    def transit(p):
        @pl.when(same)
        def _():
            for i in range(2):
                k = far0 + i
                wait_t(i, p)

                @pl.when(inner)
                def _():
                    pass_copy(k, p).start()
                cross_copy(k, p).start()

        @pl.when(jnp.logical_not(same))
        def _():
            wait_t(r1 % 2, p)
            cross_copy(r1, p).start()

    def take_far(b, p, count, fresh=False):
        for n in range(count):
            if p + n < LANE:
                wait_w(b, p + n)
            else:
                @pl.when(jnp.logical_not(hub | relay))
                def _():
                    wait_w(b, p + n)
        accumulate(b, p, count, fresh)

    def take_near(b, p, count, fresh=False):
        for n in range(count):
            @pl.when(jnp.logical_not(relay | (hub & (b == c))))
            def _():
                wait_w(b, p + n)
        accumulate(b, p, count, fresh)

    def hop(step):
        @pl.when(r == step)
        def _():
            for b in range(step, grid):
                up_copy(b).wait_recv()
            for b in range(step, grid):
                lost[0, b] = lost[0, b] + up_in[b]
            for b in range(step + 1, grid):
                up_copy(b).start()

        @pl.when(r == grid - 1 - step)
        def _():
            for b in range(0, grid - step):
                down_copy(b).wait_recv()
            for b in range(0, grid - step):
                lost[1, b] = lost[1, b] + down_in[b]
            for b in range(0, grid - 1 - step):
                down_copy(b).start()

    side = c % 2
    far_own, far_sib = far0 + side, far0 + 1 - side
    hub_order = [(c, 0)] + [(far0 + i, LANE + e) for e in range(extra) for i in range(2)] + [(c, p) for p in range(1, PIECES)]

    def near_relays(first, last):
        for t in range(first, min(last, len(hub_order))):
            if t < PIECES:
                relay_piece(c1, t)
            relay_piece(*hub_order[t])

    transit(0)
    near_relays(0, 1)
    transit(1)
    near_relays(1, 2)
    transit(2)
    near_relays(2, 3)
    take_far(far_sib, 0, 2, True)
    take_far(far_own, 0, 2, True)

    for p in range(2):
        wait_x(cx, p)
        x_copy(2, p).start()
    near_relays(3, 4)
    re, im = wlive[0], wlive[1]
    first = jnp.concatenate([re, im], axis=1)
    second = jnp.concatenate([-im, re], axis=1)
    for p in range(2):
        wait_x(c1, p)
        wait_x((c1 + 2) % 4, p)
    for b in range(grid):
        value = mm(xt[b, 0], first) + mm(xt[b, 1], second)
        lost[0, b] = value
        lost[1, b] = value * jnp.where(r == b, 0.0, 1.0)
    for b in range(1, grid):
        @pl.when((r == 0))
        def _():
            up_copy(b).start()

        @pl.when((r == grid - 1))
        def _():
            down_copy(grid - 1 - b).start()

    take_far(far_sib, 2, 2)
    for j in range(CHUNKS):
        sib_copy(0, far_sib, j).start()
    take_far(far_own, 2, 2)
    for j in range(CHUNKS):
        s = big(j)
        sib_copy(0, far_sib, j).wait_recv()
        value = part[far_own, s] + sib[0, s]
        top = jnp.max(jnp.abs(value), axis=0, keepdims=True)
        ratio = jnp.where(top > 0.0, 32767.0 / jnp.maximum(top, 1e-30), 0.0)
        qsend[s] = jnp.round(value * ratio).astype(jnp.int32).astype(jnp.int16)
        ssend[j] = jnp.broadcast_to(top * (1.0 / 32767.0), ssend.shape[1:])
        q_copy(j).start()
        sc_copy(j).start()
    near_relays(4, 5)
    take_near(c1, 0, 2, True)
    hop(1)
    take_near(c1, 2, 2)
    for j in range(CHUNKS):
        sib_copy(1, c1, j).start()
    near_relays(5, 6)
    take_near(c, 0, 2, True)
    hop(2)
    take_near(c, 2, 1)
    hop(3)
    take_near(c, 3, 1)

    value = lost[0, r] + lost[1, r]
    part_hi = value.astype(BF16)
    left = value - part_hi.astype(F32)
    part_mid = left.astype(BF16)
    part_lo = (left - part_mid.astype(F32)).astype(BF16)
    scale = 1.0 / math.sqrt(order)
    w0, w1 = wavelet[0] * scale, wavelet[1] * scale
    for j in range(CHUNKS):
        s = big(j)
        spread = mm(hot_row[s], part_hi) + mm(hot_row[s], part_mid) + mm(hot_row[s], part_lo)
        q_copy(j).wait_recv()
        sc_copy(j).wait_recv()
        sib_copy(1, c1, j).wait_recv()
        total = part[c, s] + sib[1, s] + qrecv[s].astype(jnp.int32).astype(F32) * srecv[j, 0:1, :]
        dead = dead_ref[s] > 0.5
        real = jnp.where(dead, spread[:, :win], total[:, :win])
        imag = jnp.where(dead, spread[:, win:], total[:, win:])
        out[0, s] = wown[0, s].astype(F32) - (w0 * real - w1 * imag)
        out[1, s] = wown[1, s].astype(F32) - (w0 * imag + w1 * real)

    for which in range(3):
        for p in range(2):
            x_copy(which, p).wait_send()
    for j in range(CHUNKS):
        sib_copy(0, far0 + 1 - side, j).wait_send()
        sib_copy(1, c1, j).wait_send()
        q_copy(j).wait_send()
        sc_copy(j).wait_send()
    for b in range(grid):
        @pl.when((b > r) & (r < grid - 1))
        def _():
            up_copy(b).wait_send()

        @pl.when((b < r) & (r > 0))
        def _():
            down_copy(b).wait_send()

    @pl.when(jnp.logical_not(hub))
    def _():
        pat.wait_send()

    @pl.when(same)
    def _():
        @pl.loop(0, PIECES)
        def _(p):
            own_copy(p, 2).wait_send()
            own_copy(p, 1).wait_send()

            @pl.when(jnp.logical_not(hub))
            def _():
                own_copy(p, 0).wait_send()

        @pl.loop(0, LANE)
        def _(p):
            for i in range(2):
                cross_copy(far0 + i, p).wait_send()

                @pl.when(inner)
                def _():
                    pass_copy(far0 + i, p).wait_send()

    @pl.when(hub)
    def _():
        for i in range(2):
            for e in range(extra):
                for which in range(2):
                    hub_copy(i, e, which).wait_send()

    @pl.when(jnp.logical_not(same))
    def _():
        @pl.loop(0, PIECES)
        def _(p):
            own_copy(p, 0).wait_send()

        @pl.loop(0, LANE)
        def _(p):
            lane_copy(p, 2).wait_send()
            lane_copy(p, 1).wait_send()
            cross_copy(r1, p).wait_send()

        @pl.when(inner)
        def _():
            @pl.loop(0, PIECES)
            def _(p):
                for i in range(2):
                    fwd_copy(own0 + i, p).wait_send()
            for i in range(2):
                for e in range(extra):
                    fwd_copy(far0 + i, LANE + e).wait_send()


def make_fused(order):
    def local(traces, recv_live, missing, wavelet):
        tile = traces.shape[1]
        grid, dead_n = missing.shape
        win = 128
        recv = recv_live.reshape(-1, win)
        dma, vmem = pltpu.SemaphoreType.DMA, pltpu.VMEM
        block = (2, tile, win)
        wide = (tile, 2 * win)
        scratch = [
            vmem((2, tile, tile), BF16),
            vmem(block, BF16), vmem(block, BF16), vmem(block, BF16),
            vmem((grid,) + block, BF16), vmem((2,) + block, BF16),
            vmem((2, dead_n, win), BF16), vmem((2, dead_n, win), BF16),
            vmem((grid,) + wide, F32), vmem((2,) + wide, F32),
            vmem(wide, jnp.int16), vmem(wide, jnp.int16),
            vmem((CHUNKS, 8, 2 * win), F32), vmem((CHUNKS, 8, 2 * win), F32),
            vmem((grid, 2, dead_n, tile), BF16),
            vmem((2, grid, dead_n, 2 * win), F32),
            vmem((grid, dead_n, 2 * win), F32), vmem((grid, dead_n, 2 * win), F32),
            vmem((dead_n, tile), BF16), vmem((tile, dead_n), BF16), vmem((tile, win), F32), vmem((tile, win), F32),
            dma((2,)), dma((1,)), dma((1,)), dma((3, 2)), dma((grid, 2)),
            dma((grid, PIECES)), dma((2, LANE)), dma((3, PIECES)), dma((2, PIECES - LANE, 2)),
            dma((grid, PIECES)), dma((2, LANE, 2)),
            dma((grid,)), dma((grid,)), dma((grid,)), dma((grid,)),
            dma((2, CHUNKS)), dma((2, CHUNKS)),
            dma((CHUNKS,)), dma((CHUNKS,)), dma((CHUNKS,)), dma((CHUNKS,)),
        ]
        whole = pl.BlockSpec(memory_space=pltpu.VMEM)
        return pl.pallas_call(
            functools.partial(fused_kernel, order),
            out_shape=jax.ShapeDtypeStruct(block, F32),
            in_specs=[
                pl.BlockSpec(memory_space=pl.ANY), whole, whole,
                pl.BlockSpec(memory_space=pltpu.SMEM),
            ],
            out_specs=whole,
            scratch_shapes=scratch,
            compiler_params=pltpu.CompilerParams(
                collective_id=0, has_side_effects=True, vmem_limit_bytes=56 * 2**20
            ),
        )(traces, recv, missing, wavelet)

    return local


def solution(mesh):
    in_specs = (P("freq", "row", "col"), P("freq"), P("freq", None), P("freq"))
    out_specs = P("freq", "row", "col")
    small = mesh.shape["row"] == 4 and mesh.shape["col"] == 4

    def run(traces, recv_live, missing, wavelet):
        local = (make_fused if small else make_local)(traces.shape[1])
        return jax.shard_map(
            local, mesh=mesh, in_specs=in_specs, out_specs=out_specs, check_vma=False
        )(traces, recv_live, missing, wavelet)

    return run
```

```python
import functools
import math

import jax
import jax.numpy as jnp
from jax import lax
from jax.experimental import pallas as pl
from jax.experimental.pallas import tpu as pltpu
from jax.sharding import PartitionSpec as P

F32 = jnp.float32
BF16 = jnp.bfloat16


def dot(first, second, dims=((1,), (0,)), **kw):
    return lax.dot_general(first, second, (dims, ((), ())), preferred_element_type=F32, **kw)


def make_local(order):
    def local(traces, recv_live, missing, wavelet):
        tile = traces.shape[1]
        grid = lax.axis_size("row")
        win = 128
        row = lax.axis_index("row")
        col = lax.axis_index("col")
        positions = jnp.arange(tile, dtype=jnp.int32)
        raw = traces[:, :, :win]
        gathered = lax.all_gather(raw, "row", axis=0, tiled=False)

        miss_row = lax.dynamic_index_in_dim(missing, row, 0, keepdims=False)
        miss_col = lax.dynamic_index_in_dim(missing, col, 0, keepdims=False)
        hot_row = positions[None, :] == miss_row[:, None]
        hot_col = positions[None, :] == miss_col[:, None]
        dead_row = jnp.any(hot_row, axis=0)
        dead_col = jnp.any(hot_col, axis=0)
        dead_win = jnp.any(missing[:, :, None] == positions[None, None, :win], axis=1)
        recv = (recv_live == 1).reshape(grid, tile)
        recv_row = lax.dynamic_index_in_dim(recv, row, 0, keepdims=False)
        recv_col = lax.dynamic_index_in_dim(recv, col, 0, keepdims=False)
        recv_miss_row = jnp.any(hot_row & recv_row[None, :], axis=1)
        recv_miss_col = jnp.any(hot_col & recv_col[None, :], axis=1)
        hot_row_b = hot_row.astype(BF16)
        hot_col_b = hot_col.astype(BF16)
        zero = jnp.zeros((), BF16)

        outgoing = jnp.stack([dot(hot_col_b, traces[p], ((1,), (1,))) for p in range(2)]).astype(BF16)
        route = [(r * grid + c, c * grid + r) for r in range(grid) for c in range(grid)]
        incoming = lax.ppermute(outgoing, ("row", "col"), route)
        dead_gather = lax.all_gather(outgoing[:, :, :win], "row", axis=0, tiled=False)

        swapped = lax.all_to_all(gathered, "col", split_axis=0, concat_axis=0, tiled=True)
        wide = jnp.transpose(swapped, (1, 2, 0, 3)).reshape(2, tile, grid * win)
        live_win = recv[:, :win].reshape(-1)
        keep = jnp.where(live_win[None, :] & ~dead_col[:, None], True, False)
        deads = jnp.transpose(dead_gather, (1, 2, 0, 3)).reshape(2, -1, grid * win)
        dead_keep = recv_miss_col[:, None] & ~dead_win.reshape(-1)[None, :]
        deads = jnp.where(dead_keep[None], deads, zero)
        window = [
            jnp.where(keep, wide[p], dot(hot_col_b, deads[p], ((0,), (0,))).astype(BF16))
            for p in range(2)
        ]
        masked = [jnp.where(recv_col[:, None], w, zero) for w in window]
        patched = jnp.where(recv_miss_row[None, :, None] & ~dead_col[None, None, :], incoming, zero)

        def product(left, right):
            first = jnp.concatenate([right[0], right[1]], axis=1)
            second = jnp.concatenate([-right[1], right[0]], axis=1)
            return dot(left[0], first) + dot(left[1], second)

        live = product(traces, masked)
        lost = product(patched, window)
        lost = dot(hot_row.astype(F32), lost, ((0,), (0,)), precision=lax.Precision.HIGHEST)
        partial = jnp.where(dead_row[:, None], lost, live)
        partial = jnp.transpose(partial.reshape(tile, 2, grid, win), (2, 1, 0, 3))
        total = lax.psum_scatter(partial, "col", scatter_dimension=0, tiled=True)[0]
        scale = 1.0 / math.sqrt(order)
        real = (wavelet[0] * total[0] - wavelet[1] * total[1]) * scale
        imag = (wavelet[0] * total[1] + wavelet[1] * total[0]) * scale
        own_in = lax.dynamic_index_in_dim(recv[:, :win], col, 0, keepdims=False)
        own_dead = jnp.where(
            recv_miss_row[None, :, None] & ~dead_col[None, None, :win], incoming[:, :, :win], zero
        )
        own = [
            jnp.where(
                dead_row[:, None],
                dot(hot_row_b, own_dead[p], ((0,), (0,))),
                jnp.where(own_in[None, :], raw[p], zero).astype(F32),
            )
            for p in range(2)
        ]
        return jnp.stack([own[0] - real, own[1] - imag])

    return local


MESH = pl.DeviceIdType.MESH
PIECES = 3
LANE = 2
CHUNKS = 3


def nt(first, second):
    return lax.dot_general(first, second, (((1,), (1,)), ((), ())), preferred_element_type=F32)


def mm(first, second):
    return jnp.dot(first, second, preferred_element_type=F32)


def fused_kernel(
    order, traces, recv, miss, wavelet, out,
    tile_ref, ws, wown, wlive, wbuf, tbuf, psend, precv, part, sib, qsend, qrecv, ssend, srecv,
    xt, lost, up_in, down_in, hot_col, hot_row, dead_ref, recv_rows,
    tile_sem, pat_s, pat_r, x_s, x_r, w_r, t_r, own_s, hub_s, fwd_s, tran_s,
    up_s, up_r, down_s, down_r, sib_s, sib_r, q_s, q_r, sc_s, sc_r,
):
    f = lax.axis_index("freq")
    r = lax.axis_index("row")
    c = lax.axis_index("col")
    grid = 4
    tile, win = tile_ref.shape[1], wown.shape[2]
    dead_n = xt.shape[2]
    rows = tile // PIECES
    extra = PIECES - LANE
    chunk = tile // CHUNKS
    rh, ch = r // 2, c // 2
    same = rh == ch
    hub = r == c
    inner = (r == 1) | (r == 2)
    r1 = r + 1 - 2 * (r % 2)
    c1 = c + 1 - 2 * (c % 2)
    cx = (c + 2) % 4
    mid_of_r = 2 - rh
    near_edge = 3 * rh
    far0 = 2 * (1 - ch)
    own0 = 2 * ch

    def sub(p):
        return pl.ds(pl.multiple_of(p * rows, rows), rows)

    def big(j):
        return pl.ds(pl.multiple_of(j * chunk, chunk), chunk)

    def rc(src, dst, ssem, rsem, dev):
        return pltpu.make_async_remote_copy(
            src_ref=src, dst_ref=dst, send_sem=ssem, recv_sem=rsem,
            device_id=(f, dev[0], dev[1]), device_id_type=MESH,
        )

    def own_copy(p, which):
        dev = [(r, r), (r1, r), (mid_of_r, r)][which]
        return rc(ws.at[:, sub(p)], wbuf.at[c, :, sub(p)], own_s.at[which, p], w_r.at[c, p], dev)

    def lane_copy(p, which):
        dev = [None, (r1, c), (mid_of_r, c)][which]
        slot = r % 2
        return rc(ws.at[:, sub(p)], tbuf.at[slot, :, sub(p)], own_s.at[which, p], t_r.at[slot, p], dev)

    def hub_copy(i, e, which):
        b, p = far0 + i, LANE + e
        dev = [(r1, r), (mid_of_r, r)][which]
        return rc(wbuf.at[b, :, sub(p)], wbuf.at[b, :, sub(p)], hub_s.at[i, e, which], w_r.at[b, p], dev)

    def fwd_copy(b, p):
        return rc(wbuf.at[b, :, sub(p)], wbuf.at[b, :, sub(p)], fwd_s.at[b, p], w_r.at[b, p], (near_edge, c))

    def cross_copy(k, p):
        slot = k % 2
        return rc(tbuf.at[slot, :, sub(p)], wbuf.at[c, :, sub(p)], tran_s.at[slot, p, 0], w_r.at[c, p], (r, k))

    def pass_copy(k, p):
        slot = k % 2
        return rc(tbuf.at[slot, :, sub(p)], tbuf.at[slot, :, sub(p)], tran_s.at[slot, p, 1], t_r.at[slot, p], (near_edge, c))

    def wait_w(b, p):
        rc(wbuf.at[b, :, sub(p)], wbuf.at[b, :, sub(p)], fwd_s.at[b, p], w_r.at[b, p], (r, c1)).wait_recv()

    def wait_t(slot, p):
        rc(tbuf.at[slot, :, sub(p)], tbuf.at[slot, :, sub(p)], tran_s.at[slot, p, 0], t_r.at[slot, p], (r, c1)).wait_recv()

    def x_copy(which, p):
        src = [c, c, cx][which]
        dev = [(r, c1), (r, cx), (r, c1)][which]
        return rc(xt.at[src, p], xt.at[src, p], x_s.at[which, p], x_r.at[src, p], dev)

    def wait_x(b, p):
        rc(xt.at[b, p], xt.at[b, p], x_s.at[0, p], x_r.at[b, p], (r, c1)).wait_recv()

    def up_copy(b):
        return rc(lost.at[0, b], up_in.at[b], up_s.at[b], up_r.at[b], (jnp.minimum(r + 1, grid - 1), c))

    def down_copy(b):
        return rc(lost.at[1, b], down_in.at[b], down_s.at[b], down_r.at[b], (jnp.maximum(r - 1, 0), c))

    def sib_copy(phase, b, j):
        return rc(part.at[b, big(j)], sib.at[phase, big(j)], sib_s.at[phase, j], sib_r.at[phase, j], (r, c1))

    def q_copy(j):
        return rc(qsend.at[big(j)], qrecv.at[big(j)], q_s.at[j], q_r.at[j], (r, cx))

    def sc_copy(j):
        return rc(ssend.at[j], srecv.at[j], sc_s.at[j], sc_r.at[j], (r, cx))

    pat = rc(psend, precv, pat_s.at[0], pat_r.at[0], (c, r))

    head = pltpu.make_async_copy(traces.at[:, pl.ds(0, win)], tile_ref.at[:, pl.ds(0, win)], tile_sem.at[0])
    rest = pltpu.make_async_copy(
        traces.at[:, pl.ds(win, tile - win)], tile_ref.at[:, pl.ds(win, tile - win)], tile_sem.at[1])
    head.start()
    rest.start()
    barrier = pltpu.get_barrier_semaphore()
    for n in range(1, grid * grid):
        other = (r * grid + c + n) % (grid * grid)
        pl.semaphore_signal(
            barrier, inc=1, device_id=(f, other // grid, other % grid), device_id_type=MESH)

    span = tile // win

    def lanes_of(block):
        return [recv[pl.ds(block * span + j, 1), :] for j in range(span)]

    def column(row):
        shape = (dead_n, dead_n)
        diagonal = lax.broadcasted_iota(jnp.int32, shape, 0) == lax.broadcasted_iota(jnp.int32, shape, 1)
        return jnp.sum(jnp.where(diagonal, jnp.broadcast_to(row, shape), 0), axis=1, keepdims=True)

    miss_row = miss[pl.ds(r, 1), :]
    recv_c = lanes_of(c)
    miss_c = column(miss[pl.ds(c, 1), :])
    place = lax.broadcasted_iota(jnp.int32, (dead_n, win), 1)
    for j in range(span):
        hot_col[:, j * win:(j + 1) * win] = jnp.where(
            (place + j * win == miss_c) & (recv_c[j] == 1), 1.0, 0.0).astype(BF16)
    head_hot = jnp.where(place == column(miss_row), 1.0, 0.0)
    live_q = 1.0 - jnp.max(head_hot, axis=0, keepdims=True)
    recv_q = jnp.where(recv_c[0] == 1, 1.0, 0.0)

    head.wait()
    for p in range(2):
        psend[p] = (nt(hot_col[...], tile_ref[p, :win, :]) * live_q).astype(BF16)
    pl.semaphore_wait(barrier, grid * grid - 1)

    @pl.when(hub)
    def _():
        precv[...] = psend[...]

    @pl.when(jnp.logical_not(hub))
    def _():
        pat.start()

    recv_r = lanes_of(r)
    for j in range(span):
        lane = jnp.where(recv_r[j] == 1, 1.0, 0.0)
        recv_rows[pl.ds(j * win, win), :] = jnp.transpose(jnp.broadcast_to(lane, (win, win)))
    ones = jnp.ones((dead_n, win), BF16)
    for j in range(CHUNKS):
        spot = lax.broadcasted_iota(jnp.int32, (chunk, dead_n), 0) + j * chunk
        hot = jnp.where(spot == miss_row, 1.0, 0.0).astype(BF16)
        hot_row[pl.ds(j * chunk, chunk), :] = hot
        dead_ref[pl.ds(j * chunk, chunk), :] = mm(hot, ones)
    rest.wait()
    for p in range(2):
        for j in range(CHUNKS):
            s = pl.ds(j * chunk, chunk)
            raw = tile_ref[p, s, :win].astype(F32) * recv_q
            wlive[p, s] = jnp.where(dead_ref[s] > 0.5, 0.0, raw).astype(BF16)

    @pl.when(jnp.logical_not(hub))
    def _():
        pat.wait_recv()

    for p in range(2):
        for j in range(CHUNKS):
            s = pl.ds(j * chunk, chunk)
            full = wlive[p, s].astype(F32) + mm(hot_row[s], precv[p])
            wown[p, s] = full.astype(BF16)
            ws[p, s] = (full * recv_rows[s]).astype(BF16)

    @pl.when(hub)
    def _():
        wbuf[c] = ws[...]

    @pl.when(same & jnp.logical_not(hub))
    def _():
        @pl.loop(0, PIECES)
        def _(p):
            own_copy(p, 2).start()
            own_copy(p, 1).start()
            own_copy(p, 0).start()

    @pl.when(jnp.logical_not(same))
    def _():
        @pl.loop(LANE, PIECES)
        def _(p):
            own_copy(p, 0).start()

        @pl.loop(0, LANE)
        def _(p):
            lane_copy(p, 2).start()
            lane_copy(p, 1).start()
            own_copy(p, 0).start()


    for p in range(2):
        for j in range(CHUNKS):
            s = pl.ds(j * chunk, chunk)
            xt[c, p, :, s] = nt(hot_col[...], tile_ref[p, s, :]).astype(BF16)
        x_copy(1, p).start()
        x_copy(0, p).start()

    @pl.when(hub)
    def _():
        own_copy(0, 2).start()
        own_copy(0, 1).start()
        for e in range(extra):
            for i in range(2):
                wait_w(far0 + i, LANE + e)
                for which in range(2):
                    hub_copy(i, e, which).start()

        @pl.loop(1, PIECES)
        def _(p):
            own_copy(p, 2).start()
            own_copy(p, 1).start()

    relay = inner & jnp.logical_not(same)

    def accumulate(b, p, count, fresh=False):
        k = pl.ds(pl.multiple_of(p * rows, rows), count * rows)
        re, im = wbuf[b, 0, k, :], wbuf[b, 1, k, :]
        first = jnp.concatenate([re, im], axis=1)
        second = jnp.concatenate([-im, re], axis=1)

        @pl.loop(0, CHUNKS)
        def _(j):
            s = big(j)
            value = mm(tile_ref[0, s, k], first) + mm(tile_ref[1, s, k], second)
            part[b, s] = value if fresh else part[b, s] + value

    def relay_piece(b, p):
        @pl.when(relay)
        def _():
            wait_w(b, p)
            fwd_copy(b, p).start()

    def transit(p):
        @pl.when(same)
        def _():
            for i in range(2):
                k = far0 + i
                wait_t(i, p)

                @pl.when(inner)
                def _():
                    pass_copy(k, p).start()
                cross_copy(k, p).start()

        @pl.when(jnp.logical_not(same))
        def _():
            wait_t(r1 % 2, p)
            cross_copy(r1, p).start()

    def take_far(b, p, count, fresh=False):
        for n in range(count):
            if p + n < LANE:
                wait_w(b, p + n)
            else:
                @pl.when(jnp.logical_not(hub | relay))
                def _():
                    wait_w(b, p + n)
        accumulate(b, p, count, fresh)

    def take_near(b, p, count, fresh=False):
        for n in range(count):
            @pl.when(jnp.logical_not(relay | (hub & (b == c))))
            def _():
                wait_w(b, p + n)
        accumulate(b, p, count, fresh)

    def hop(step):
        @pl.when(r == step)
        def _():
            for b in range(step, grid):
                up_copy(b).wait_recv()
            for b in range(step, grid):
                lost[0, b] = lost[0, b] + up_in[b]
            for b in range(step + 1, grid):
                up_copy(b).start()

        @pl.when(r == grid - 1 - step)
        def _():
            for b in range(0, grid - step):
                down_copy(b).wait_recv()
            for b in range(0, grid - step):
                lost[1, b] = lost[1, b] + down_in[b]
            for b in range(0, grid - 1 - step):
                down_copy(b).start()

    side = c % 2
    far_own, far_sib = far0 + side, far0 + 1 - side
    hub_order = [(c, 0)] + [(far0 + i, LANE + e) for e in range(extra) for i in range(2)] + [(c, p) for p in range(1, PIECES)]

    def near_relays(first, last):
        for t in range(first, min(last, len(hub_order))):
            if t < PIECES:
                relay_piece(c1, t)
            relay_piece(*hub_order[t])

    transit(0)
    near_relays(0, 1)
    transit(1)
    near_relays(1, 2)
    near_relays(2, 3)
    take_far(far_sib, 0, 1, True)
    take_far(far_own, 0, 1, True)

    for p in range(2):
        wait_x(cx, p)
        x_copy(2, p).start()
    near_relays(3, 4)
    re, im = wlive[0], wlive[1]
    first = jnp.concatenate([re, im], axis=1)
    second = jnp.concatenate([-im, re], axis=1)
    for p in range(2):
        wait_x(c1, p)
        wait_x((c1 + 2) % 4, p)
    for b in range(grid):
        value = mm(xt[b, 0], first) + mm(xt[b, 1], second)
        lost[0, b] = value
        lost[1, b] = value * jnp.where(r == b, 0.0, 1.0)
    for b in range(1, grid):
        @pl.when((r == 0))
        def _():
            up_copy(b).start()

        @pl.when((r == grid - 1))
        def _():
            down_copy(grid - 1 - b).start()

    take_far(far_sib, 1, 2)
    for j in range(CHUNKS):
        sib_copy(0, far_sib, j).start()
    take_far(far_own, 1, 2)
    for j in range(CHUNKS):
        s = big(j)
        sib_copy(0, far_sib, j).wait_recv()
        value = part[far_own, s] + sib[0, s]
        top = jnp.max(jnp.abs(value), axis=0, keepdims=True)
        ratio = jnp.where(top > 0.0, 32767.0 / jnp.maximum(top, 1e-30), 0.0)
        qsend[s] = jnp.round(value * ratio).astype(jnp.int32).astype(jnp.int16)
        ssend[j] = jnp.broadcast_to(top * (1.0 / 32767.0), ssend.shape[1:])
        q_copy(j).start()
        sc_copy(j).start()
    near_relays(4, 5)
    take_near(c1, 0, 1, True)
    hop(1)
    take_near(c1, 1, 2)
    for j in range(CHUNKS):
        sib_copy(1, c1, j).start()
    near_relays(5, 6)
    take_near(c, 0, 1, True)
    hop(2)
    take_near(c, 1, 1)
    hop(3)
    take_near(c, 2, 1)

    value = lost[0, r] + lost[1, r]
    part_hi = value.astype(BF16)
    left = value - part_hi.astype(F32)
    part_mid = left.astype(BF16)
    part_lo = (left - part_mid.astype(F32)).astype(BF16)
    scale = 1.0 / math.sqrt(order)
    w0, w1 = wavelet[0] * scale, wavelet[1] * scale
    for j in range(CHUNKS):
        s = big(j)
        spread = mm(hot_row[s], part_hi) + mm(hot_row[s], part_mid) + mm(hot_row[s], part_lo)
        q_copy(j).wait_recv()
        sc_copy(j).wait_recv()
        sib_copy(1, c1, j).wait_recv()
        total = part[c, s] + sib[1, s] + qrecv[s].astype(jnp.int32).astype(F32) * srecv[j, 0:1, :]
        dead = dead_ref[s] > 0.5
        real = jnp.where(dead, spread[:, :win], total[:, :win])
        imag = jnp.where(dead, spread[:, win:], total[:, win:])
        out[0, s] = wown[0, s].astype(F32) - (w0 * real - w1 * imag)
        out[1, s] = wown[1, s].astype(F32) - (w0 * imag + w1 * real)

    for which in range(3):
        for p in range(2):
            x_copy(which, p).wait_send()
    for j in range(CHUNKS):
        sib_copy(0, far0 + 1 - side, j).wait_send()
        sib_copy(1, c1, j).wait_send()
        q_copy(j).wait_send()
        sc_copy(j).wait_send()
    for b in range(grid):
        @pl.when((b > r) & (r < grid - 1))
        def _():
            up_copy(b).wait_send()

        @pl.when((b < r) & (r > 0))
        def _():
            down_copy(b).wait_send()

    @pl.when(jnp.logical_not(hub))
    def _():
        pat.wait_send()

    @pl.when(same)
    def _():
        @pl.loop(0, PIECES)
        def _(p):
            own_copy(p, 2).wait_send()
            own_copy(p, 1).wait_send()

            @pl.when(jnp.logical_not(hub))
            def _():
                own_copy(p, 0).wait_send()

        @pl.loop(0, LANE)
        def _(p):
            for i in range(2):
                cross_copy(far0 + i, p).wait_send()

                @pl.when(inner)
                def _():
                    pass_copy(far0 + i, p).wait_send()

    @pl.when(hub)
    def _():
        for i in range(2):
            for e in range(extra):
                for which in range(2):
                    hub_copy(i, e, which).wait_send()

    @pl.when(jnp.logical_not(same))
    def _():
        @pl.loop(0, PIECES)
        def _(p):
            own_copy(p, 0).wait_send()

        @pl.loop(0, LANE)
        def _(p):
            lane_copy(p, 2).wait_send()
            lane_copy(p, 1).wait_send()
            cross_copy(r1, p).wait_send()

        @pl.when(inner)
        def _():
            @pl.loop(0, PIECES)
            def _(p):
                for i in range(2):
                    fwd_copy(own0 + i, p).wait_send()
            for i in range(2):
                for e in range(extra):
                    fwd_copy(far0 + i, LANE + e).wait_send()


def make_fused(order):
    def local(traces, recv_live, missing, wavelet):
        tile = traces.shape[1]
        grid, dead_n = missing.shape
        win = 128
        recv = recv_live.reshape(-1, win)
        dma, vmem = pltpu.SemaphoreType.DMA, pltpu.VMEM
        block = (2, tile, win)
        wide = (tile, 2 * win)
        scratch = [
            vmem((2, tile, tile), BF16),
            vmem(block, BF16), vmem(block, BF16), vmem(block, BF16),
            vmem((grid,) + block, BF16), vmem((2,) + block, BF16),
            vmem((2, dead_n, win), BF16), vmem((2, dead_n, win), BF16),
            vmem((grid,) + wide, F32), vmem((2,) + wide, F32),
            vmem(wide, jnp.int16), vmem(wide, jnp.int16),
            vmem((CHUNKS, 8, 2 * win), F32), vmem((CHUNKS, 8, 2 * win), F32),
            vmem((grid, 2, dead_n, tile), BF16),
            vmem((2, grid, dead_n, 2 * win), F32),
            vmem((grid, dead_n, 2 * win), F32), vmem((grid, dead_n, 2 * win), F32),
            vmem((dead_n, tile), BF16), vmem((tile, dead_n), BF16), vmem((tile, win), F32), vmem((tile, win), F32),
            dma((2,)), dma((1,)), dma((1,)), dma((3, 2)), dma((grid, 2)),
            dma((grid, PIECES)), dma((2, LANE)), dma((3, PIECES)), dma((2, PIECES - LANE, 2)),
            dma((grid, PIECES)), dma((2, LANE, 2)),
            dma((grid,)), dma((grid,)), dma((grid,)), dma((grid,)),
            dma((2, CHUNKS)), dma((2, CHUNKS)),
            dma((CHUNKS,)), dma((CHUNKS,)), dma((CHUNKS,)), dma((CHUNKS,)),
        ]
        whole = pl.BlockSpec(memory_space=pltpu.VMEM)
        return pl.pallas_call(
            functools.partial(fused_kernel, order),
            out_shape=jax.ShapeDtypeStruct(block, F32),
            in_specs=[
                pl.BlockSpec(memory_space=pl.ANY), whole, whole,
                pl.BlockSpec(memory_space=pltpu.SMEM),
            ],
            out_specs=whole,
            scratch_shapes=scratch,
            compiler_params=pltpu.CompilerParams(
                collective_id=0, has_side_effects=True, vmem_limit_bytes=56 * 2**20
            ),
        )(traces, recv, missing, wavelet)

    return local


def solution(mesh):
    in_specs = (P("freq", "row", "col"), P("freq"), P("freq", None), P("freq"))
    out_specs = P("freq", "row", "col")
    small = mesh.shape["row"] == 4 and mesh.shape["col"] == 4

    def run(traces, recv_live, missing, wavelet):
        local = (make_fused if small else make_local)(traces.shape[1])
        return jax.shard_map(
            local, mesh=mesh, in_specs=in_specs, out_specs=out_specs, check_vma=False
        )(traces, recv_live, missing, wavelet)

    return run
```

```python
import functools
import math

import jax
import jax.numpy as jnp
from jax import lax
from jax.experimental import pallas as pl
from jax.experimental.pallas import tpu as pltpu
from jax.sharding import PartitionSpec as P

F32 = jnp.float32
BF16 = jnp.bfloat16


def dot(first, second, dims=((1,), (0,)), **kw):
    return lax.dot_general(first, second, (dims, ((), ())), preferred_element_type=F32, **kw)


def make_local(order):
    def local(traces, recv_live, missing, wavelet):
        tile = traces.shape[1]
        grid = lax.axis_size("row")
        win = 128
        row = lax.axis_index("row")
        col = lax.axis_index("col")
        positions = jnp.arange(tile, dtype=jnp.int32)
        raw = traces[:, :, :win]
        gathered = lax.all_gather(raw, "row", axis=0, tiled=False)

        miss_row = lax.dynamic_index_in_dim(missing, row, 0, keepdims=False)
        miss_col = lax.dynamic_index_in_dim(missing, col, 0, keepdims=False)
        hot_row = positions[None, :] == miss_row[:, None]
        hot_col = positions[None, :] == miss_col[:, None]
        dead_row = jnp.any(hot_row, axis=0)
        dead_col = jnp.any(hot_col, axis=0)
        dead_win = jnp.any(missing[:, :, None] == positions[None, None, :win], axis=1)
        recv = (recv_live == 1).reshape(grid, tile)
        recv_row = lax.dynamic_index_in_dim(recv, row, 0, keepdims=False)
        recv_col = lax.dynamic_index_in_dim(recv, col, 0, keepdims=False)
        recv_miss_row = jnp.any(hot_row & recv_row[None, :], axis=1)
        recv_miss_col = jnp.any(hot_col & recv_col[None, :], axis=1)
        hot_row_b = hot_row.astype(BF16)
        hot_col_b = hot_col.astype(BF16)
        zero = jnp.zeros((), BF16)

        outgoing = jnp.stack([dot(hot_col_b, traces[p], ((1,), (1,))) for p in range(2)]).astype(BF16)
        route = [(r * grid + c, c * grid + r) for r in range(grid) for c in range(grid)]
        incoming = lax.ppermute(outgoing, ("row", "col"), route)
        dead_gather = lax.all_gather(outgoing[:, :, :win], "row", axis=0, tiled=False)

        swapped = lax.all_to_all(gathered, "col", split_axis=0, concat_axis=0, tiled=True)
        wide = jnp.transpose(swapped, (1, 2, 0, 3)).reshape(2, tile, grid * win)
        live_win = recv[:, :win].reshape(-1)
        keep = jnp.where(live_win[None, :] & ~dead_col[:, None], True, False)
        deads = jnp.transpose(dead_gather, (1, 2, 0, 3)).reshape(2, -1, grid * win)
        dead_keep = recv_miss_col[:, None] & ~dead_win.reshape(-1)[None, :]
        deads = jnp.where(dead_keep[None], deads, zero)
        window = [
            jnp.where(keep, wide[p], dot(hot_col_b, deads[p], ((0,), (0,))).astype(BF16))
            for p in range(2)
        ]
        masked = [jnp.where(recv_col[:, None], w, zero) for w in window]
        patched = jnp.where(recv_miss_row[None, :, None] & ~dead_col[None, None, :], incoming, zero)

        def product(left, right):
            first = jnp.concatenate([right[0], right[1]], axis=1)
            second = jnp.concatenate([-right[1], right[0]], axis=1)
            return dot(left[0], first) + dot(left[1], second)

        live = product(traces, masked)
        lost = product(patched, window)
        lost = dot(hot_row.astype(F32), lost, ((0,), (0,)), precision=lax.Precision.HIGHEST)
        partial = jnp.where(dead_row[:, None], lost, live)
        partial = jnp.transpose(partial.reshape(tile, 2, grid, win), (2, 1, 0, 3))
        total = lax.psum_scatter(partial, "col", scatter_dimension=0, tiled=True)[0]
        scale = 1.0 / math.sqrt(order)
        real = (wavelet[0] * total[0] - wavelet[1] * total[1]) * scale
        imag = (wavelet[0] * total[1] + wavelet[1] * total[0]) * scale
        own_in = lax.dynamic_index_in_dim(recv[:, :win], col, 0, keepdims=False)
        own_dead = jnp.where(
            recv_miss_row[None, :, None] & ~dead_col[None, None, :win], incoming[:, :, :win], zero
        )
        own = [
            jnp.where(
                dead_row[:, None],
                dot(hot_row_b, own_dead[p], ((0,), (0,))),
                jnp.where(own_in[None, :], raw[p], zero).astype(F32),
            )
            for p in range(2)
        ]
        return jnp.stack([own[0] - real, own[1] - imag])

    return local


MESH = pl.DeviceIdType.MESH
PIECES = 3
LANE = 2
CHUNKS = 3


def nt(first, second):
    return lax.dot_general(first, second, (((1,), (1,)), ((), ())), preferred_element_type=F32)


def mm(first, second):
    return jnp.dot(first, second, preferred_element_type=F32)


def fused_kernel(
    order, traces, recv, miss, wavelet, out,
    tile_ref, ws, wown, wlive, wbuf, tbuf, psend, precv, part, sib, qsend, qrecv, ssend, srecv,
    xt, lost, up_in, down_in, hot_col, hot_row, dead_ref, recv_rows,
    tile_sem, pat_s, pat_r, x_s, x_r, w_r, t_r, own_s, hub_s, fwd_s, tran_s,
    up_s, up_r, down_s, down_r, sib_s, sib_r, q_s, q_r, sc_s, sc_r,
):
    f = lax.axis_index("freq")
    r = lax.axis_index("row")
    c = lax.axis_index("col")
    grid = 4
    tile, win = tile_ref.shape[1], wown.shape[2]
    dead_n = xt.shape[2]
    rows = tile // PIECES
    extra = PIECES - LANE
    chunk = tile // CHUNKS
    rh, ch = r // 2, c // 2
    same = rh == ch
    hub = r == c
    inner = (r == 1) | (r == 2)
    r1 = r + 1 - 2 * (r % 2)
    c1 = c + 1 - 2 * (c % 2)
    cx = (c + 2) % 4
    mid_of_r = 2 - rh
    near_edge = 3 * rh
    far0 = 2 * (1 - ch)
    own0 = 2 * ch

    def sub(p):
        return pl.ds(pl.multiple_of(p * rows, rows), rows)

    def big(j):
        return pl.ds(pl.multiple_of(j * chunk, chunk), chunk)

    def rc(src, dst, ssem, rsem, dev):
        return pltpu.make_async_remote_copy(
            src_ref=src, dst_ref=dst, send_sem=ssem, recv_sem=rsem,
            device_id=(f, dev[0], dev[1]), device_id_type=MESH,
        )

    def own_copy(p, which):
        dev = [(r, r), (r1, r), (mid_of_r, r)][which]
        return rc(ws.at[:, sub(p)], wbuf.at[c, :, sub(p)], own_s.at[which, p], w_r.at[c, p], dev)

    def lane_copy(p, which):
        dev = [None, (r1, c), (mid_of_r, c)][which]
        slot = r % 2
        return rc(ws.at[:, sub(p)], tbuf.at[slot, :, sub(p)], own_s.at[which, p], t_r.at[slot, p], dev)

    def hub_copy(i, e, which):
        b, p = far0 + i, LANE + e
        dev = [(r1, r), (mid_of_r, r)][which]
        return rc(wbuf.at[b, :, sub(p)], wbuf.at[b, :, sub(p)], hub_s.at[i, e, which], w_r.at[b, p], dev)

    def fwd_copy(b, p):
        return rc(wbuf.at[b, :, sub(p)], wbuf.at[b, :, sub(p)], fwd_s.at[b, p], w_r.at[b, p], (near_edge, c))

    def cross_copy(k, p):
        slot = k % 2
        return rc(tbuf.at[slot, :, sub(p)], wbuf.at[c, :, sub(p)], tran_s.at[slot, p, 0], w_r.at[c, p], (r, k))

    def pass_copy(k, p):
        slot = k % 2
        return rc(tbuf.at[slot, :, sub(p)], tbuf.at[slot, :, sub(p)], tran_s.at[slot, p, 1], t_r.at[slot, p], (near_edge, c))

    def wait_w(b, p):
        rc(wbuf.at[b, :, sub(p)], wbuf.at[b, :, sub(p)], fwd_s.at[b, p], w_r.at[b, p], (r, c1)).wait_recv()

    def wait_t(slot, p):
        rc(tbuf.at[slot, :, sub(p)], tbuf.at[slot, :, sub(p)], tran_s.at[slot, p, 0], t_r.at[slot, p], (r, c1)).wait_recv()

    def x_copy(which, p):
        src = [c, c, cx][which]
        dev = [(r, c1), (r, cx), (r, c1)][which]
        return rc(xt.at[src, p], xt.at[src, p], x_s.at[which, p], x_r.at[src, p], dev)

    def wait_x(b, p):
        rc(xt.at[b, p], xt.at[b, p], x_s.at[0, p], x_r.at[b, p], (r, c1)).wait_recv()

    def up_copy(b):
        return rc(lost.at[0, b], up_in.at[b], up_s.at[b], up_r.at[b], (jnp.minimum(r + 1, grid - 1), c))

    def down_copy(b):
        return rc(lost.at[1, b], down_in.at[b], down_s.at[b], down_r.at[b], (jnp.maximum(r - 1, 0), c))

    def sib_copy(phase, b, j):
        return rc(part.at[b, big(j)], sib.at[phase, big(j)], sib_s.at[phase, j], sib_r.at[phase, j], (r, c1))

    def q_copy(j):
        return rc(qsend.at[big(j)], qrecv.at[big(j)], q_s.at[j], q_r.at[j], (r, cx))

    def sc_copy(j):
        return rc(ssend.at[j], srecv.at[j], sc_s.at[j], sc_r.at[j], (r, cx))

    pat = rc(psend, precv, pat_s.at[0], pat_r.at[0], (c, r))

    head = pltpu.make_async_copy(traces.at[:, pl.ds(0, win)], tile_ref.at[:, pl.ds(0, win)], tile_sem.at[0])
    rest = pltpu.make_async_copy(
        traces.at[:, pl.ds(win, tile - win)], tile_ref.at[:, pl.ds(win, tile - win)], tile_sem.at[1])
    head.start()
    rest.start()
    barrier = pltpu.get_barrier_semaphore()
    for n in range(1, grid * grid):
        other = (r * grid + c + n) % (grid * grid)
        pl.semaphore_signal(
            barrier, inc=1, device_id=(f, other // grid, other % grid), device_id_type=MESH)

    span = tile // win

    def lanes_of(block):
        return [recv[pl.ds(block * span + j, 1), :] for j in range(span)]

    def column(row):
        shape = (dead_n, dead_n)
        diagonal = lax.broadcasted_iota(jnp.int32, shape, 0) == lax.broadcasted_iota(jnp.int32, shape, 1)
        return jnp.sum(jnp.where(diagonal, jnp.broadcast_to(row, shape), 0), axis=1, keepdims=True)

    miss_row = miss[pl.ds(r, 1), :]
    recv_c = lanes_of(c)
    miss_c = column(miss[pl.ds(c, 1), :])
    place = lax.broadcasted_iota(jnp.int32, (dead_n, win), 1)
    for j in range(span):
        hot_col[:, j * win:(j + 1) * win] = jnp.where(
            (place + j * win == miss_c) & (recv_c[j] == 1), 1.0, 0.0).astype(BF16)
    head_hot = jnp.where(place == column(miss_row), 1.0, 0.0)
    live_q = 1.0 - jnp.max(head_hot, axis=0, keepdims=True)
    recv_q = jnp.where(recv_c[0] == 1, 1.0, 0.0)

    head.wait()
    for p in range(2):
        psend[p] = (nt(hot_col[...], tile_ref[p, :win, :]) * live_q).astype(BF16)
    pl.semaphore_wait(barrier, grid * grid - 1)

    @pl.when(hub)
    def _():
        precv[...] = psend[...]

    @pl.when(jnp.logical_not(hub))
    def _():
        pat.start()

    recv_r = lanes_of(r)
    for j in range(span):
        lane = jnp.where(recv_r[j] == 1, 1.0, 0.0)
        recv_rows[pl.ds(j * win, win), :] = jnp.transpose(jnp.broadcast_to(lane, (win, win)))
    ones = jnp.ones((dead_n, win), BF16)
    for j in range(CHUNKS):
        spot = lax.broadcasted_iota(jnp.int32, (chunk, dead_n), 0) + j * chunk
        hot = jnp.where(spot == miss_row, 1.0, 0.0).astype(BF16)
        hot_row[pl.ds(j * chunk, chunk), :] = hot
        dead_ref[pl.ds(j * chunk, chunk), :] = mm(hot, ones)
    rest.wait()
    for p in range(2):
        for j in range(CHUNKS):
            s = pl.ds(j * chunk, chunk)
            raw = tile_ref[p, s, :win].astype(F32) * recv_q
            wlive[p, s] = jnp.where(dead_ref[s] > 0.5, 0.0, raw).astype(BF16)

    @pl.when(jnp.logical_not(hub))
    def _():
        pat.wait_recv()

    for p in range(2):
        for j in range(CHUNKS):
            s = pl.ds(j * chunk, chunk)
            full = wlive[p, s].astype(F32) + mm(hot_row[s], precv[p])
            wown[p, s] = full.astype(BF16)
            ws[p, s] = (full * recv_rows[s]).astype(BF16)

    @pl.when(hub)
    def _():
        wbuf[c] = ws[...]

    @pl.when(same & jnp.logical_not(hub))
    def _():
        @pl.loop(0, PIECES)
        def _(p):
            own_copy(p, 2).start()
            own_copy(p, 1).start()
            own_copy(p, 0).start()

    @pl.when(jnp.logical_not(same))
    def _():
        @pl.loop(LANE, PIECES)
        def _(p):
            own_copy(p, 0).start()

        @pl.loop(0, LANE)
        def _(p):
            lane_copy(p, 2).start()
            lane_copy(p, 1).start()
            own_copy(p, 0).start()


    for p in range(2):
        for j in range(CHUNKS):
            s = pl.ds(j * chunk, chunk)
            xt[c, p, :, s] = nt(hot_col[...], tile_ref[p, s, :]).astype(BF16)
        x_copy(1, p).start()
        x_copy(0, p).start()

    @pl.when(hub)
    def _():
        own_copy(0, 2).start()
        own_copy(0, 1).start()
        for e in range(extra):
            for i in range(2):
                wait_w(far0 + i, LANE + e)
                for which in range(2):
                    hub_copy(i, e, which).start()

        @pl.loop(1, PIECES)
        def _(p):
            own_copy(p, 2).start()
            own_copy(p, 1).start()

    relay = inner & jnp.logical_not(same)

    def accumulate(b, p, count, fresh=False):
        k = pl.ds(pl.multiple_of(p * rows, rows), count * rows)
        re, im = wbuf[b, 0, k, :], wbuf[b, 1, k, :]
        first = jnp.concatenate([re, im], axis=1)
        second = jnp.concatenate([-im, re], axis=1)

        @pl.loop(0, CHUNKS)
        def _(j):
            s = big(j)
            value = mm(tile_ref[0, s, k], first) + mm(tile_ref[1, s, k], second)
            part[b, s] = value if fresh else part[b, s] + value

    def relay_piece(b, p):
        @pl.when(relay)
        def _():
            wait_w(b, p)
            fwd_copy(b, p).start()

    def transit(p):
        @pl.when(same)
        def _():
            for i in range(2):
                k = far0 + i
                wait_t(i, p)

                @pl.when(inner)
                def _():
                    pass_copy(k, p).start()
                cross_copy(k, p).start()

        @pl.when(jnp.logical_not(same))
        def _():
            wait_t(r1 % 2, p)
            cross_copy(r1, p).start()

    def take_far(b, p, count, fresh=False):
        for n in range(count):
            if p + n < LANE:
                wait_w(b, p + n)
            else:
                @pl.when(jnp.logical_not(hub | relay))
                def _():
                    wait_w(b, p + n)
        accumulate(b, p, count, fresh)

    def take_near(b, p, count, fresh=False):
        for n in range(count):
            @pl.when(jnp.logical_not(relay | (hub & (b == c))))
            def _():
                wait_w(b, p + n)
        accumulate(b, p, count, fresh)

    def hop(step):
        @pl.when(r == step)
        def _():
            for b in range(step, grid):
                up_copy(b).wait_recv()
            for b in range(step, grid):
                lost[0, b] = lost[0, b] + up_in[b]
            for b in range(step + 1, grid):
                up_copy(b).start()

        @pl.when(r == grid - 1 - step)
        def _():
            for b in range(0, grid - step):
                down_copy(b).wait_recv()
            for b in range(0, grid - step):
                lost[1, b] = lost[1, b] + down_in[b]
            for b in range(0, grid - 1 - step):
                down_copy(b).start()

    side = c % 2
    far_own, far_sib = far0 + side, far0 + 1 - side
    hub_order = [(c, 0)] + [(far0 + i, LANE + e) for e in range(extra) for i in range(2)] + [(c, p) for p in range(1, PIECES)]

    def near_relays(first, last):
        for t in range(first, min(last, len(hub_order))):
            if t < PIECES:
                relay_piece(c1, t)
            relay_piece(*hub_order[t])

    transit(0)
    near_relays(0, 1)
    transit(1)
    near_relays(1, 2)
    near_relays(2, 3)
    take_far(far_sib, 0, 1, True)
    take_far(far_own, 0, 1, True)

    for p in range(2):
        wait_x(cx, p)
        x_copy(2, p).start()
    near_relays(3, 4)
    re, im = wlive[0], wlive[1]
    first = jnp.concatenate([re, im], axis=1)
    second = jnp.concatenate([-im, re], axis=1)
    for p in range(2):
        wait_x(c1, p)
        wait_x((c1 + 2) % 4, p)
    for b in range(grid):
        value = mm(xt[b, 0], first) + mm(xt[b, 1], second)
        lost[0, b] = value
        lost[1, b] = value * jnp.where(r == b, 0.0, 1.0)
    for b in range(1, grid):
        @pl.when((r == 0))
        def _():
            up_copy(b).start()

        @pl.when((r == grid - 1))
        def _():
            down_copy(grid - 1 - b).start()

    take_far(far_sib, 1, 2)
    for j in range(CHUNKS):
        sib_copy(0, far_sib, j).start()
    take_far(far_own, 1, 2)
    for j in range(CHUNKS):
        s = big(j)
        sib_copy(0, far_sib, j).wait_recv()
        value = part[far_own, s] + sib[0, s]
        top = jnp.max(jnp.abs(value), axis=0, keepdims=True)
        ratio = jnp.where(top > 0.0, 32767.0 / jnp.maximum(top, 1e-30), 0.0)
        qsend[s] = jnp.round(value * ratio).astype(jnp.int32).astype(jnp.int16)
        ssend[j] = jnp.broadcast_to(top * (1.0 / 32767.0), ssend.shape[1:])
        q_copy(j).start()
        sc_copy(j).start()
    near_relays(4, 5)
    hop(1)
    take_near(c1, 0, 3, True)
    for j in range(CHUNKS):
        sib_copy(1, c1, j).start()
    near_relays(5, 6)
    hop(2)
    take_near(c, 0, 2, True)
    hop(3)
    take_near(c, 2, 1)

    value = lost[0, r] + lost[1, r]
    part_hi = value.astype(BF16)
    left = value - part_hi.astype(F32)
    part_mid = left.astype(BF16)
    part_lo = (left - part_mid.astype(F32)).astype(BF16)
    scale = 1.0 / math.sqrt(order)
    w0, w1 = wavelet[0] * scale, wavelet[1] * scale
    for j in range(CHUNKS):
        s = big(j)
        spread = mm(hot_row[s], part_hi) + mm(hot_row[s], part_mid) + mm(hot_row[s], part_lo)
        q_copy(j).wait_recv()
        sc_copy(j).wait_recv()
        sib_copy(1, c1, j).wait_recv()
        total = part[c, s] + sib[1, s] + qrecv[s].astype(jnp.int32).astype(F32) * srecv[j, 0:1, :]
        dead = dead_ref[s] > 0.5
        real = jnp.where(dead, spread[:, :win], total[:, :win])
        imag = jnp.where(dead, spread[:, win:], total[:, win:])
        out[0, s] = wown[0, s].astype(F32) - (w0 * real - w1 * imag)
        out[1, s] = wown[1, s].astype(F32) - (w0 * imag + w1 * real)

    for which in range(3):
        for p in range(2):
            x_copy(which, p).wait_send()
    for j in range(CHUNKS):
        sib_copy(0, far0 + 1 - side, j).wait_send()
        sib_copy(1, c1, j).wait_send()
        q_copy(j).wait_send()
        sc_copy(j).wait_send()
    for b in range(grid):
        @pl.when((b > r) & (r < grid - 1))
        def _():
            up_copy(b).wait_send()

        @pl.when((b < r) & (r > 0))
        def _():
            down_copy(b).wait_send()

    @pl.when(jnp.logical_not(hub))
    def _():
        pat.wait_send()

    @pl.when(same)
    def _():
        @pl.loop(0, PIECES)
        def _(p):
            own_copy(p, 2).wait_send()
            own_copy(p, 1).wait_send()

            @pl.when(jnp.logical_not(hub))
            def _():
                own_copy(p, 0).wait_send()

        @pl.loop(0, LANE)
        def _(p):
            for i in range(2):
                cross_copy(far0 + i, p).wait_send()

                @pl.when(inner)
                def _():
                    pass_copy(far0 + i, p).wait_send()

    @pl.when(hub)
    def _():
        for i in range(2):
            for e in range(extra):
                for which in range(2):
                    hub_copy(i, e, which).wait_send()

    @pl.when(jnp.logical_not(same))
    def _():
        @pl.loop(0, PIECES)
        def _(p):
            own_copy(p, 0).wait_send()

        @pl.loop(0, LANE)
        def _(p):
            lane_copy(p, 2).wait_send()
            lane_copy(p, 1).wait_send()
            cross_copy(r1, p).wait_send()

        @pl.when(inner)
        def _():
            @pl.loop(0, PIECES)
            def _(p):
                for i in range(2):
                    fwd_copy(own0 + i, p).wait_send()
            for i in range(2):
                for e in range(extra):
                    fwd_copy(far0 + i, LANE + e).wait_send()


def make_fused(order):
    def local(traces, recv_live, missing, wavelet):
        tile = traces.shape[1]
        grid, dead_n = missing.shape
        win = 128
        recv = recv_live.reshape(-1, win)
        dma, vmem = pltpu.SemaphoreType.DMA, pltpu.VMEM
        block = (2, tile, win)
        wide = (tile, 2 * win)
        scratch = [
            vmem((2, tile, tile), BF16),
            vmem(block, BF16), vmem(block, BF16), vmem(block, BF16),
            vmem((grid,) + block, BF16), vmem((2,) + block, BF16),
            vmem((2, dead_n, win), BF16), vmem((2, dead_n, win), BF16),
            vmem((grid,) + wide, F32), vmem((2,) + wide, F32),
            vmem(wide, jnp.int16), vmem(wide, jnp.int16),
            vmem((CHUNKS, 8, 2 * win), F32), vmem((CHUNKS, 8, 2 * win), F32),
            vmem((grid, 2, dead_n, tile), BF16),
            vmem((2, grid, dead_n, 2 * win), F32),
            vmem((grid, dead_n, 2 * win), F32), vmem((grid, dead_n, 2 * win), F32),
            vmem((dead_n, tile), BF16), vmem((tile, dead_n), BF16), vmem((tile, win), F32), vmem((tile, win), F32),
            dma((2,)), dma((1,)), dma((1,)), dma((3, 2)), dma((grid, 2)),
            dma((grid, PIECES)), dma((2, LANE)), dma((3, PIECES)), dma((2, PIECES - LANE, 2)),
            dma((grid, PIECES)), dma((2, LANE, 2)),
            dma((grid,)), dma((grid,)), dma((grid,)), dma((grid,)),
            dma((2, CHUNKS)), dma((2, CHUNKS)),
            dma((CHUNKS,)), dma((CHUNKS,)), dma((CHUNKS,)), dma((CHUNKS,)),
        ]
        whole = pl.BlockSpec(memory_space=pltpu.VMEM)
        return pl.pallas_call(
            functools.partial(fused_kernel, order),
            out_shape=jax.ShapeDtypeStruct(block, F32),
            in_specs=[
                pl.BlockSpec(memory_space=pl.ANY), whole, whole,
                pl.BlockSpec(memory_space=pltpu.SMEM),
            ],
            out_specs=whole,
            scratch_shapes=scratch,
            compiler_params=pltpu.CompilerParams(
                collective_id=0, has_side_effects=True, vmem_limit_bytes=56 * 2**20
            ),
        )(traces, recv, missing, wavelet)

    return local


def solution(mesh):
    in_specs = (P("freq", "row", "col"), P("freq"), P("freq", None), P("freq"))
    out_specs = P("freq", "row", "col")
    small = mesh.shape["row"] == 4 and mesh.shape["col"] == 4

    def run(traces, recv_live, missing, wavelet):
        local = (make_fused if small else make_local)(traces.shape[1])
        return jax.shard_map(
            local, mesh=mesh, in_specs=in_specs, out_specs=out_specs, check_vma=False
        )(traces, recv_live, missing, wavelet)

    return run
```
